256 devices in a mesh: seq: 16 (over y, x_lo, core), fsdp: 16 (over z, x_hi).
Axes of the slice: x: 4 (x_hi: 2, x_lo: 2; x = x_hi * 2 + x_lo), y: 4, z: 8, core: 2. Of those that a mesh axis runs over, the one named last changes fastest.
Arguments:
- clean_states: bfloat16 [16, 4096, 4096], P('fsdp', 'seq'), may hold values from -6 to 6
- noise_mask: int32 [16, 4096], P('fsdp', 'seq'), may hold values from 0 to 1, as said below
- mask_embed: bfloat16 [4096], replicated, may hold values from -6 to 6
- queries: bfloat16 [16, 4096, 2048], P('fsdp', 'seq'), may hold values from -96 to 96
- w_key: bfloat16 [4096, 512], P('fsdp'), may hold values from -0.09375 to 0.09375
- w_value: bfloat16 [4096, 512], P('fsdp'), may hold values from -0.09375 to 0.09375
Outputs:
- noisy_attention: bfloat16 [16, 4096, 2048], P('fsdp', 'seq')
The draws below stay inside these ranges and needn't reach their ends.
Inputs may be any that keep to these rules, and one draw needn't show every extreme that they name: `noise_mask`: each block of 256 positions has its own masking rate; 1 marks a masked position.
All inputs are finite; a program needn't handle non-finite values.
Results may differ from the reference program's by a relative error of at most 0.011.
Values may be sent and summed in bfloat16 or wider, within the bound.
A program may use at most 64 MiB of HBM per device.

```python
import jax
import jax.numpy as jnp
from jax import lax

D = 4096
HEADS = 16
KV_HEADS = 4
HEAD_DIM = 128
BLOCK = 256
LEN = 4096
SEQS = 16


def draw_noise_mask(key, part):
    key_levels, key_ticks = jax.random.split(jax.random.fold_in(key, 11))
    levels = jax.random.randint(key_levels, (SEQS, LEN // BLOCK, 1), 0, 65)
    ticks = jax.random.randint(key_ticks, (SEQS, LEN // BLOCK, BLOCK), 0, 64)
    return (ticks < levels).astype(jnp.int32).reshape(SEQS, LEN)


def draw_queries(key, part):
    key_base = jax.random.fold_in(jax.random.fold_in(key, 23), 0)
    shape = (SEQS, LEN, HEADS * HEAD_DIM)
    return jnp.clip(jax.random.normal(key_base, shape, jnp.float32) * 3.0, -18.0, 18.0).astype(jnp.bfloat16)


def steps_of(stream_key, extent, cuts, low, top_value):
    gain, own = 1.0, jax.random.fold_in(stream_key, 6)
    for position, shards_of in cuts:
        heights = jnp.exp(jax.random.uniform(jax.random.fold_in(own, position), (shards_of,), jnp.float32, low / len(cuts), top_value / len(cuts)))
        gain = gain * jnp.repeat(heights, extent[position] // shards_of).reshape([-1 if axis == position else 1 for axis in range(len(extent))])
    return gain


def gaussian(rng, extent, deviation, limit, cuts=(), kind=jnp.bfloat16):
    entries = deviation * jax.random.normal(rng, extent, jnp.float32)
    if cuts:
        entries = entries * steps_of(rng, extent, cuts, -0.22, 0.18)
    return jnp.clip(entries, -limit, limit).astype(kind)


def setup_inputs(seed: int = 0) -> dict:
    key_list = jax.random.split(jax.random.key(seed), 7)
    return {
        "clean_states": gaussian(key_list[0], (SEQS, LEN, D), 1.0, 6.0, ((0, 16), (1, 16))),
        "noise_mask": draw_noise_mask(jax.random.fold_in(key_list[6], 71), 0),
        "mask_embed": gaussian(key_list[2], (D,), 1.0, 6.0),
        "queries": draw_queries(jax.random.fold_in(key_list[6], 71), 0),
        "w_key": gaussian(key_list[4], (D, KV_HEADS * HEAD_DIM), D ** -0.5, 0.09375, ((0, 16),)),
        "w_value": gaussian(key_list[5], (D, KV_HEADS * HEAD_DIM), D ** -0.5, 0.09375, ((0, 16),)),
    }


ROPE_BASE = 500000.0


def rotate(key_rows, positions):
    half_dim = key_rows.shape[-1] // 2
    frequency = ROPE_BASE ** (-(jnp.arange(half_dim, dtype=jnp.float32) * 2.0 / key_rows.shape[-1]))
    angles = positions[:, None] * frequency[None, :]
    cosine = jnp.cos(angles)[:, None, :]
    sine_part = jnp.sin(angles)[:, None, :]
    first_half = key_rows[..., :half_dim]
    second_half = key_rows[..., half_dim:]
    return jnp.concatenate([first_half * cosine - second_half * sine_part, second_half * cosine + first_half * sine_part], -1)


def reference(clean_states, noise_mask, mask_embed, queries, w_key, w_value):
    length = clean_states.shape[1]
    kv_width = w_key.shape[1]
    kv_count = kv_width // HEAD_DIM
    groups = HEADS // kv_count
    blocks = length // BLOCK
    positions = jnp.arange(length, dtype=jnp.int32)
    score_scale = HEAD_DIM ** -0.5

    def one_sequence(inputs):
        states, noise_marks, query_rows = inputs
        noisy_rows = jnp.where(noise_marks[:, None] == 1, mask_embed[None, :], states)
        both_rows = jnp.concatenate([states, noisy_rows], 0)
        key_sums = jnp.dot(both_rows, w_key, preferred_element_type=jnp.float32).reshape(2 * length, kv_count, HEAD_DIM)
        both_positions = jnp.concatenate([positions, positions]).astype(jnp.float32)
        key_rows = rotate(key_sums, both_positions).astype(jnp.bfloat16)
        value_rows = jnp.dot(both_rows, w_value, preferred_element_type=jnp.float32).astype(jnp.bfloat16).reshape(2 * length, kv_count, HEAD_DIM)
        key_rows, value_rows = lax.optimization_barrier((key_rows, value_rows))
        clean_keys = key_rows[:length].astype(jnp.float32)
        clean_values = value_rows[:length].astype(jnp.float32)
        noisy_keys = key_rows[length:].reshape(blocks, BLOCK, kv_count, HEAD_DIM)
        noisy_values = value_rows[length:].reshape(blocks, BLOCK, kv_count, HEAD_DIM)
        query_blocks = query_rows.reshape(blocks, BLOCK, kv_count, groups, HEAD_DIM)

        def one_block(inner):
            block_index, block_queries, own_keys, own_values = inner
            all_keys = jnp.concatenate([clean_keys, own_keys.astype(jnp.float32)], 0)
            all_values = jnp.concatenate([clean_values, own_values.astype(jnp.float32)], 0)
            scores = jnp.einsum('qkgd,tkd->qkgt', block_queries.astype(jnp.float32), all_keys) * score_scale
            allowed = jnp.concatenate([positions // BLOCK < block_index, jnp.ones((BLOCK,), bool)])
            scores = jnp.where(allowed[None, None, None, :], scores, -1e30)
            row_max = jnp.max(scores, -1, keepdims=True)
            probs = jnp.where(allowed[None, None, None, :], jnp.exp(scores - row_max), 0.0)
            row_total = jnp.sum(probs, -1)
            rounded = lax.optimization_barrier(probs.astype(jnp.bfloat16))
            mixture = jnp.einsum('qkgt,tkd->qkgd', rounded.astype(jnp.float32), all_values)
            return (mixture / row_total[..., None]).astype(jnp.bfloat16).reshape(BLOCK, kv_count * groups * HEAD_DIM)

        outputs = lax.map(one_block, (jnp.arange(blocks, dtype=jnp.int32), query_blocks, noisy_keys, noisy_values))
        return outputs.reshape(length, kv_count * groups * HEAD_DIM)

    return lax.map(one_sequence, (clean_states, noise_mask, queries))
```

```python
import jax
import jax.numpy as jnp
import numpy as np
from jax import lax
from jax.experimental import pallas as pl
from jax.experimental.pallas import tpu as pltpu
from jax.sharding import PartitionSpec as P

MESH = pl.DeviceIdType.MESH
BF16 = jnp.bfloat16
F32 = jnp.float32
HEAD_DIM = 128
BLOCK = 256
ROPE_BASE = 500000.0
SCORE_SCALE = float(HEAD_DIM**-0.5 * np.log2(np.e))
NT = (((1,), (1,)), ((), ()))

ROUTE = {
    (0, 1, 0): "y+", (0, 1, 1): "y-", (1, 1, 0): "xl", (1, 1, 1): "y+",
    (0, 2, 0): "y-", (0, 2, 1): "xl", (1, 2, 0): "xh", (1, 2, 1): "xh",
    (0, 3, 0): "y+", (0, 3, 1): "y-", (1, 3, 0): "xl", (1, 3, 1): "y+",
    (0, 4, 0): "y-", (0, 4, 1): "xl", (1, 4, 0): "y-", (1, 4, 1): "xl",
}
OPPOSITE = {"y+": "y-", "y-": "y+", "xl": "xl", "xh": "xh"}
KV_ORDER = ((0, 1), (1, 0), (3, 0), (1, 1), (3, 1), (2, 0), (2, 1))

EV_X, EV_XH, EV_Z, EV_P = 0, 1, 3, 19
EV_Q, EV_M, EV_K, EV_V, EV_O = 35, 38, 41, 49, 57
EV_COUNT = 60


def event(ring, distance, other):
    return (ring * 4 + distance - 1) * 2 + other


def kernel(
    states, marks, mask_row, queries, w_key, w_value, cosine, sine, far_cosine, far_sine, out,
    x_buf, w_buf, sums, k_own, v_own, k_all, v_all, q_buf, m_buf, o_buf,
    tables, row_max, mix, send_sem, recv_sem, local_sem,
):
    seq = lax.axis_index("seq")
    fsdp = lax.axis_index("fsdp")
    core = seq % 2
    chip = seq // 2
    xl = chip % 2
    y = chip // 2
    z = fsdp // 2
    xh = fsdp % 2
    role = y % 2
    side = (y + xl) % 2
    mate = (3 - y) * 2 + xl

    def at(yy, xx, cc):
        return ((yy % 4 * 2 + xx) * 2 + cc, fsdp)

    near = {
        "y+": at(y + 1, xl, core),
        "y-": at(y + 3, xl, core),
        "xl": at(y, 1 - xl, core),
        "xh": (at(y, 1 - xl, core)[0], z * 2 + 1 - xh),
        "z+": (seq, (z + 1) % 8 * 2 + xh),
        "z-": (seq, (z + 7) % 8 * 2 + xh),
        "core": at(y, xl, 1 - core),
        "mate": at(3 - y, xl, core),
        "mate2": at(3 - y, xl, 1 - core),
    }

    def remote(src, dst, number, device):
        return pltpu.make_async_remote_copy(
            src, dst, send_sem.at[number], recv_sem.at[number],
            device_id=device, device_id_type=MESH,
        )

    locals_ = []

    def local(src, dst, number):
        copy = pltpu.make_async_copy(src, dst, local_sem.at[number])
        copy.start()
        return copy

    wide = pl.ds(pl.multiple_of(core * 256, 256), 256)
    own = fsdp * 2
    load_w = []
    for half in range(2):
        rows = pl.ds(half * 128, 128)
        load_w.append(local(w_key.at[rows, wide], w_buf.at[own + half, :, pl.ds(0, 256)], half * 2))
        load_w.append(local(w_value.at[rows, wide], w_buf.at[own + half, :, pl.ds(256, 256)], half * 2 + 1))
    my_rows = pl.ds(pl.multiple_of(core * 256, 256), 256)
    load_x = local(states, x_buf.at[my_rows, :], 4)
    head = 2 * core + role
    q_cols = pl.ds(pl.multiple_of(head * 512, 512), 512)
    load_q = local(queries.at[:, q_cols], q_buf.at[core], 5)
    load_t = []
    for number, table in enumerate((cosine, sine)):
        load_t.append(local(table, tables.at[number], 6 + number))

    peers = [at(y + dy, xl if dx == 0 else 1 - xl, core) for dy, dx in KV_ORDER]
    peers += [near["core"], near["mate2"], near["xh"], near["z+"], near["z-"]]
    barrier = pltpu.get_barrier_semaphore()
    for peer in peers:
        pl.semaphore_signal(barrier, inc=1, device_id=peer, device_id_type=MESH)
    pl.semaphore_wait(barrier, len(peers))

    sends = []

    def send(src, dst, number, device):
        copy = remote(src, dst, number, device)
        copy.start()
        sends.append(copy)

    for copy in load_w:
        copy.wait()
    other = (z * 2 + 1 - xh) * 2

    def piece(zz, flip, half):
        aa = 1 - xh if flip else xh
        return (zz % 8 * 2 + aa) * 2 + half

    def part(distance, ring):
        if distance < 4:
            return pl.ds(0, 128)
        return pl.ds(ring * 64, 64)

    def ring_send(ring, distance, flip):
        source = z - (distance - 1) if ring == 0 else z + (distance - 1)
        ref = w_buf.at[piece(source + 8, flip, side), part(distance, ring), :]
        send(ref, ref, EV_Z + event(ring, distance, flip), near["z+" if ring == 0 else "z-"])

    send(w_buf.at[own + 1 - side], w_buf.at[own + 1 - side], EV_XH, near["xh"])
    for ring in range(2):
        ring_send(ring, 1, 0)
    send(w_buf.at[own + side], w_buf.at[own + side], EV_XH + 1, near["xh"])
    send(states, x_buf.at[my_rows, :], EV_X, near["core"])

    x_buf[pl.ds(512, 16), :] = jnp.broadcast_to(mask_row[...], (16, mask_row.shape[1]))
    flags = jnp.broadcast_to(marks[...].astype(F32), (128, 256))
    m_buf[core] = jnp.transpose(flags).astype(BF16)
    v_all[:, pl.ds(128, 128)] = jnp.ones((v_all.shape[0], 128), BF16)
    row_max[...] = jnp.full(row_max.shape, -1e30, F32)
    mix[...] = jnp.zeros(mix.shape, F32)

    for copy in load_t:
        copy.wait()
    near_c, near_s = tables[0], tables[1]
    for pair, where in ((1, mate), (0, chip)):
        far_c, far_s = far_cosine[pl.ds(where, 1), :], far_sine[pl.ds(where, 1), :]
        tables[pair * 2] = near_c * far_c - near_s * far_s
        tables[pair * 2 + 1] = near_s * far_c + near_c * far_s

    landing = w_buf.at[other + side]
    remote(landing, landing, EV_XH, near["xh"]).wait_recv()
    for ring in range(2):
        ring_send(ring, 1, 1)

    def q_at(kv_head):
        return queries.at[:, pl.ds(pl.multiple_of(kv_head * 512, 512), 512)]

    send(q_at(2 * (1 - core) + role), q_buf.at[core], EV_Q, near["core"])
    send(m_buf.at[core], m_buf.at[core], EV_M, near["core"])
    send(m_buf.at[core], m_buf.at[2 + core], EV_M + 1, near["mate"])
    send(m_buf.at[core], m_buf.at[2 + core], EV_M + 2, near["mate2"])

    load_x.wait()
    theirs = x_buf.at[pl.ds(pl.multiple_of((1 - core) * 256, 256), 256), :]
    remote(theirs, theirs, EV_X, near["core"]).wait_recv()
    landing = w_buf.at[other + 1 - side]
    remote(landing, landing, EV_XH + 1, near["xh"]).wait_recv()

    def project(zz, first=False):
        zz = zz % 8
        weights = w_buf[pl.ds(zz * 4, 4)].reshape(512, 512)
        rows = x_buf[:, pl.ds(pl.multiple_of(zz * 512, 512), 512)]
        term = jnp.dot(rows, weights, preferred_element_type=F32)
        if first:
            sums[...] = term
        else:
            sums[...] += term

    project(z, True)

    def plane_wait(distance):
        for ring in range(2):
            source = z - distance if ring == 0 else z + distance
            for flip in range(2):
                way = ROUTE[ring, distance, flip]
                ref = w_buf.at[piece(source + 8, flip, 1 - side), part(distance, ring), :]
                remote(ref, ref, EV_P + event(ring, distance, flip), near[OPPOSITE[way]]).wait_recv()

    for distance in range(1, 5):
        for flip in range(2):
            for ring in range(2):
                source = z - distance if ring == 0 else z + distance
                ref = w_buf.at[piece(source + 8, flip, side), part(distance, ring), :]
                number = event(ring, distance, flip)
                remote(ref, ref, EV_Z + number, near["z-" if ring == 0 else "z+"]).wait_recv()
                if distance < 4:
                    ring_send(ring, distance + 1, flip)
                way = ROUTE[ring, distance, flip]
                if way != "xh":
                    send(ref, ref, EV_P + number, near[way])
                elif flip == 1:
                    for mine in range(2):
                        ref = w_buf.at[piece(source + 8, 1 - mine, side), part(distance, ring), :]
                        send(ref, ref, EV_P + event(ring, distance, mine), near["xh"])
        if distance == 1:
            send(q_at(2 * core + 1 - role), q_buf.at[2 + core], EV_Q + 1, near["mate"])
            send(q_at(2 * (1 - core) + 1 - role), q_buf.at[2 + core], EV_Q + 2, near["mate2"])
        else:
            plane_wait(distance - 1)
            project(z + 8 - distance + 1)
            project(z + distance - 1)
    plane_wait(4)
    project(z + 4)

    def rotate(rows, pair, first, count):
        turned = pltpu.roll(rows, 64, 1)
        span = pl.ds(first, count)
        return rows * tables[pair * 2, span, :] + turned * tables[pair * 2 + 1, span, :]

    for kind in range(2):
        keys = sums[pl.ds(0, 512), pl.ds(kind * 128, 128)]
        k_own[kind] = rotate(keys, 0, 0, 512).astype(BF16)
        v_own[kind] = sums[pl.ds(0, 512), pl.ds(256 + kind * 128, 128)].astype(BF16)

    def kv_rows(where):
        return pl.ds(pl.multiple_of(where * 512, 512), 512)

    def k_at(where):
        return k_all.at[kv_rows(where), :]

    def v_at(where):
        return v_all.at[kv_rows(where), pl.ds(0, 128)]

    for dy, dx in KV_ORDER:
        device = at(y + dy, xl if dx == 0 else 1 - xl, core)
        kind = (role + dy) % 2
        send(k_own.at[kind], k_at(chip), EV_K + dy * 2 + dx, device)
        send(v_own.at[kind], v_at(chip), EV_V + dy * 2 + dx, device)
    k_all[kv_rows(chip), :] = k_own[role]
    v_all[kv_rows(chip), pl.ds(0, 128)] = v_own[role]

    load_q.wait()
    for number, slot, device in (
        (EV_Q, 1 - core, near["core"]),
        (EV_Q + 1, 2 + core, near["mate"]),
        (EV_Q + 2, 3 - core, near["mate2"]),
    ):
        remote(q_buf.at[slot], q_buf.at[slot], number, device).wait_recv()
        mark = number - EV_Q + EV_M
        remote(m_buf.at[slot], m_buf.at[slot], mark, device).wait_recv()

    mask_key = sums[pl.ds(512, 16), pl.ds(pl.multiple_of(role * 128, 128), 128)]
    mask_value = sums[pl.ds(512, 16), pl.ds(pl.multiple_of(256 + role * 128, 128), 128)]
    mask_key = jnp.broadcast_to(mask_key[0:1, :], (256, 128))
    mask_value = jnp.broadcast_to(mask_value[0:1, :], (256, 128)).astype(BF16).astype(F32)

    def build(pair, quad):
        for i in range(2):
            slot = pair * 2 + i
            mine = 2 * xl + i
            base = 4096 + slot * 1024
            block = pl.multiple_of((quad * 4 + mine) * 256, 256)
            masked = m_buf[slot].astype(F32) > 0.5
            noisy_k = jnp.where(
                masked,
                rotate(mask_key, pair, i * 256, 256),
                k_all[pl.ds(block, 256), :].astype(F32),
            ).astype(BF16)
            noisy_v = jnp.where(
                masked, mask_value, v_all[pl.ds(block, 256), pl.ds(0, 128)].astype(F32)
            ).astype(BF16)
            for j in range(4):
                rows = pl.ds(base + j * 256, 256)
                start = pl.multiple_of((quad * 4 + j) * 256, 256)

                @pl.when(j < mine)
                def _():
                    k_all[rows, :] = k_all[pl.ds(start, 256), :]
                    v_all[rows, pl.ds(0, 128)] = v_all[pl.ds(start, 256), pl.ds(0, 128)]

                @pl.when(j >= mine)
                def _():
                    k_all[rows, :] = noisy_k

                @pl.when(j == mine)
                def _():
                    v_all[rows, pl.ds(0, 128)] = noisy_v

                @pl.when(j > mine)
                def _():
                    v_all[rows, :] = jnp.zeros((256, 256), BF16)

    def absorb(slot, start):
        span = pl.ds(pl.multiple_of(start, 1024), 1024)
        for g in range(4):
            query = q_buf[slot, :, pl.ds(g * 128, 128)]
            scores = lax.dot_general(query, k_all[span, :], NT, preferred_element_type=F32)
            before = row_max[slot * 4 + g]
            after = jnp.maximum(before, jnp.max(scores, 1, keepdims=True))
            shrink = jnp.exp2((before - after) * SCORE_SCALE)
            probs = jnp.exp2((scores - after[:, :1]) * SCORE_SCALE).astype(BF16)
            term = jnp.dot(probs, v_all[span, :], preferred_element_type=F32)
            for part_ in range(2):
                lanes = pl.ds(part_ * 128, 128)
                mix[slot * 4 + g, :, lanes] = (
                    mix[slot * 4 + g, :, lanes] * shrink + term[:, part_ * 128 : part_ * 128 + 128]
                )
            row_max[slot * 4 + g] = after

    def finish(slot):
        for g in range(4):
            total = mix[slot * 4 + g]
            o_buf[slot, :, pl.ds(g * 128, 128)] = (total[:, :128] / total[:, 128:]).astype(BF16)

    def wait_kv(source, dy, dx):
        where = source * 2 + (xl if dx == 0 else 1 - xl)
        device = at(source, xl if dx == 0 else 1 - xl, core)
        remote(k_at(where), k_at(where), EV_K + dy * 2 + dx, device).wait_recv()
        remote(v_at(where), v_at(where), EV_V + dy * 2 + dx, device).wait_recv()

    def step(number, carry):
        dy = jnp.where(number == 2, 3, number)
        quad = (y + 4 - dy) % 4

        @pl.when(number > 0)
        def _():
            wait_kv(quad, dy, 0)

        wait_kv(quad, dy, 1)

        @pl.when(number == 0)
        def _():
            build(0, quad)

        @pl.when(quad == 3 - y)
        def _():
            build(1, quad)

        def item(kind, carry):
            pair = jnp.where((kind == 1) | (kind == 2), 1, 0)
            level = jnp.where(pair == 1, 3 - y, y)
            active = jnp.where(kind < 2, quad == level, quad < level)

            @pl.when(active)
            def _():
                def one(i, carry):
                    slot = pair * 2 + i
                    absorb(slot, jnp.where(kind < 2, 4096 + slot * 1024, quad * 1024))
                    return carry

                lax.fori_loop(0, 2, one, 0)

            return carry

        lax.fori_loop(0, 4, item, 0)
        return carry

    lax.fori_loop(0, 3, step, 0)

    last = (y + 2) % 4
    wait_kv(last, 2, 0)
    wait_kv(last, 2, 1)
    out_cols = pl.ds(pl.multiple_of(head * 512, 512), 512)

    def final(i, carry):
        slot = (i + 2) % 4

        @pl.when(last < jnp.where(slot >= 2, 3 - y, y))
        def _():
            absorb(slot, last * 1024)

        finish(slot)

        @pl.when(slot >= 2)
        def _():
            remote(
                o_buf.at[slot], out.at[:, out_cols], EV_O + (slot - core + 2) % 2,
                at(3 - y, xl, slot % 2),
            ).start()

        return carry

    lax.fori_loop(0, 4, final, 0)
    send(o_buf.at[1 - core], out.at[:, out_cols], EV_O + 2, near["core"])
    store = local(o_buf.at[core], out.at[:, out_cols], 5)
    store.wait()

    def o_at(kv_head):
        return out.at[:, pl.ds(pl.multiple_of(kv_head * 512, 512), 512)]

    for number, kv_head, device in (
        (EV_O, 2 * core + 1 - role, near["mate"]),
        (EV_O + 1, 2 * (1 - core) + 1 - role, near["mate2"]),
        (EV_O + 2, 2 * (1 - core) + role, near["core"]),
    ):
        remote(o_at(kv_head), o_at(kv_head), number, device).wait_recv()
    for number in range(2):
        slot = 2 + (core + number) % 2
        remote(o_buf.at[slot], out.at[:, out_cols], EV_O + number, at(3 - y, xl, slot % 2)).wait_send()
    for copy in sends:
        copy.wait_send()


def tables_of(positions):
    half = HEAD_DIM // 2
    steps = np.arange(half, dtype=np.float32) * np.float32(2.0) / np.float32(HEAD_DIM)
    frequency = (np.float32(ROPE_BASE) ** (-steps)).astype(np.float64)
    angles = positions.astype(np.float64)[:, None] * frequency[None, :]
    cosine = np.cos(angles).astype(np.float32)
    sine = np.sin(angles).astype(np.float32)
    return jnp.asarray(np.concatenate([cosine, cosine], 1)), jnp.asarray(np.concatenate([-sine, sine], 1))


def solution(mesh):
    def shards(clean_states, noise_mask, mask_embed, queries, w_key, w_value):
        _, rows, width = clean_states.shape
        cosine, sine = tables_of(np.arange(2 * rows))
        far_cosine, far_sine = tables_of(np.arange(8) * 2 * rows)
        any_ = pl.BlockSpec(memory_space=pl.ANY)
        vmem = pl.BlockSpec(memory_space=pltpu.VMEM)
        output = pl.pallas_call(
            kernel,
            out_shape=jax.ShapeDtypeStruct((256, 2048), BF16),
            in_specs=[any_, vmem, vmem, any_, any_, any_, any_, any_, vmem, vmem],
            out_specs=any_,
            scratch_shapes=[
                pltpu.VMEM((528, 4096), BF16),
                pltpu.VMEM((32, 128, 512), BF16),
                pltpu.VMEM((528, 512), F32),
                pltpu.VMEM((2, 512, 128), BF16),
                pltpu.VMEM((2, 512, 128), BF16),
                pltpu.VMEM((8192, 128), BF16),
                pltpu.VMEM((8192, 256), BF16),
                pltpu.VMEM((4, 256, 512), BF16),
                pltpu.VMEM((4, 256, 128), BF16),
                pltpu.VMEM((4, 256, 512), BF16),
                pltpu.VMEM((4, 512, 128), F32),
                pltpu.VMEM((16, 256, 128), F32),
                pltpu.VMEM((16, 256, 256), F32),
                pltpu.SemaphoreType.DMA((EV_COUNT,)),
                pltpu.SemaphoreType.DMA((EV_COUNT,)),
                pltpu.SemaphoreType.DMA((10,)),
            ],
            compiler_params=pltpu.CompilerParams(
                collective_id=0, has_side_effects=True, vmem_limit_bytes=56 << 20
            ),
        )(
            clean_states[0], noise_mask, mask_embed[None, :], queries[0],
            w_key, w_value, cosine, sine, far_cosine, far_sine,
        )
        return output[None]

    placed = (
        P("fsdp", "seq", None),
        P("fsdp", "seq"),
        P(),
        P("fsdp", "seq", None),
        P("fsdp", None),
        P("fsdp", None),
    )
    return jax.shard_map(
        shards, mesh=mesh, in_specs=placed, out_specs=P("fsdp", "seq", None), check_vma=False
    )
```

```python
import jax
import jax.numpy as jnp
import numpy as np
from jax import lax
from jax.experimental import pallas as pl
from jax.experimental.pallas import tpu as pltpu
from jax.sharding import PartitionSpec as P

MESH = pl.DeviceIdType.MESH
BF16 = jnp.bfloat16
F32 = jnp.float32
HEAD_DIM = 128
BLOCK = 256
ROPE_BASE = 500000.0
SCORE_SCALE = float(HEAD_DIM**-0.5 * np.log2(np.e))
NT = (((1,), (1,)), ((), ()))

ROUTE = {
    (0, 1, 0): "buddy", (0, 1, 1): "xl", (1, 1, 0): "buddy", (1, 1, 1): "xl",
    (0, 2, 0): "buddy", (0, 2, 1): "xl", (1, 2, 0): "xh", (1, 2, 1): "xh",
    (0, 3, 0): "buddy", (0, 3, 1): "xl", (1, 3, 0): "mate", (1, 3, 1): "xl",
    (0, 4, 0): "buddy", (0, 4, 1): "xl", (1, 4, 0): "mate", (1, 4, 1): "buddy",
}
PLANE = ((0, 1), (1, 0), (3, 0), (1, 1), (3, 1), (2, 0), (2, 1))

EV_X, EV_XH, EV_Z, EV_P = 0, 1, 3, 19
EV_Q, EV_M, EV_K, EV_V, EV_O = 35, 38, 41, 49, 57
EV_COUNT = 60


def event(ring, distance, other):
    return (ring * 4 + distance - 1) * 2 + other


def kernel(
    states, marks, mask_row, queries, w_key, w_value, cosine, sine, far_cosine, far_sine, out,
    x_buf, w_buf, sums, k_own, v_own, v_relay, k_all, v_all, q_buf, m_buf, o_buf,
    tables, row_max, mix, send_sem, recv_sem, local_sem,
):
    seq = lax.axis_index("seq")
    fsdp = lax.axis_index("fsdp")
    core = seq % 2
    chip = seq // 2
    xl = chip % 2
    y = chip // 2
    z = fsdp // 2
    xh = fsdp % 2
    role = y % 2
    side = (y + xl) % 2
    mate = (3 - y) * 2 + xl

    def at(yy, xx, cc):
        return ((yy % 4 * 2 + xx) * 2 + cc, fsdp)

    near = {
        "buddy": at(y // 2 * 2 + 1 - y % 2, xl, core),
        "xl": at(y, 1 - xl, core),
        "xh": (at(y, 1 - xl, core)[0], z * 2 + 1 - xh),
        "z+": (seq, (z + 1) % 8 * 2 + xh),
        "z-": (seq, (z + 7) % 8 * 2 + xh),
        "core": at(y, xl, 1 - core),
        "mate": at(3 - y, xl, core),
        "mate2": at(3 - y, xl, 1 - core),
    }

    def remote(src, dst, number, device):
        return pltpu.make_async_remote_copy(
            src, dst, send_sem.at[number], recv_sem.at[number],
            device_id=device, device_id_type=MESH,
        )

    locals_ = []

    def local(src, dst, number):
        copy = pltpu.make_async_copy(src, dst, local_sem.at[number])
        copy.start()
        return copy

    wide = pl.ds(pl.multiple_of(core * 256, 256), 256)
    own = fsdp * 2
    load_w = []
    for half in range(2):
        rows = pl.ds(half * 128, 128)
        load_w.append(local(w_key.at[rows, wide], w_buf.at[own + half, :, pl.ds(0, 256)], half * 2))
        load_w.append(local(w_value.at[rows, wide], w_buf.at[own + half, :, pl.ds(256, 256)], half * 2 + 1))
    my_rows = pl.ds(pl.multiple_of(core * 256, 256), 256)
    load_x = local(states, x_buf.at[my_rows, :], 4)
    head = 2 * core + role
    q_cols = pl.ds(pl.multiple_of(head * 512, 512), 512)
    load_q = local(queries.at[:, q_cols], q_buf.at[core], 5)
    load_t = []
    for number, table in enumerate((cosine, sine)):
        load_t.append(local(table, tables.at[number], 6 + number))

    peers = [at(y + dy, xl if dx == 0 else 1 - xl, core) for dy, dx in PLANE]
    peers += [near["core"], near["mate2"], near["xh"], near["z+"], near["z-"]]
    barrier = pltpu.get_barrier_semaphore()
    for peer in peers:
        pl.semaphore_signal(barrier, inc=1, device_id=peer, device_id_type=MESH)
    pl.semaphore_wait(barrier, len(peers))

    sends = []

    def send(src, dst, number, device):
        copy = remote(src, dst, number, device)
        copy.start()
        sends.append(copy)

    for copy in load_w:
        copy.wait()
    other = (z * 2 + 1 - xh) * 2

    def piece(zz, flip, half):
        aa = 1 - xh if flip else xh
        return (zz % 8 * 2 + aa) * 2 + half

    def part(distance, ring):
        if distance < 4:
            return pl.ds(0, 128)
        return pl.ds(ring * 64, 64)

    def ring_send(ring, distance, flip):
        source = z - (distance - 1) if ring == 0 else z + (distance - 1)
        ref = w_buf.at[piece(source + 8, flip, side), part(distance, ring), :]
        send(ref, ref, EV_Z + event(ring, distance, flip), near["z+" if ring == 0 else "z-"])

    send(w_buf.at[own + 1 - side], w_buf.at[own + 1 - side], EV_XH, near["xh"])
    for ring in range(2):
        ring_send(ring, 1, 0)
    send(w_buf.at[own + side], w_buf.at[own + side], EV_XH + 1, near["xh"])
    send(states, x_buf.at[my_rows, :], EV_X, near["core"])

    mask_rows = mask_row[...].astype(F32)
    for i in range(32):
        wide_row = jnp.broadcast_to(mask_rows[i : i + 1, :], (16, 128))
        x_buf[pl.ds(512, 16), pl.ds(i * 128, 128)] = wide_row.astype(BF16)
    flags = jnp.broadcast_to(marks[...].astype(F32), (128, 256))
    m_buf[core] = jnp.transpose(flags).astype(BF16)
    v_all[:, pl.ds(128, 128)] = jnp.ones((v_all.shape[0], 128), BF16)
    row_max[...] = jnp.full(row_max.shape, -1e30, F32)
    mix[...] = jnp.zeros(mix.shape, F32)

    for copy in load_t:
        copy.wait()
    near_c, near_s = tables[0], tables[1]
    for pair, where in ((1, mate), (0, chip)):
        far_c, far_s = far_cosine[pl.ds(where, 1), :], far_sine[pl.ds(where, 1), :]
        tables[pair * 2] = near_c * far_c - near_s * far_s
        tables[pair * 2 + 1] = near_s * far_c + near_c * far_s

    landing = w_buf.at[other + side]
    remote(landing, landing, EV_XH, near["xh"]).wait_recv()
    for ring in range(2):
        ring_send(ring, 1, 1)

    def q_at(kv_head):
        return queries.at[:, pl.ds(pl.multiple_of(kv_head * 512, 512), 512)]

    send(q_at(2 * (1 - core) + role), q_buf.at[core], EV_Q, near["core"])
    send(m_buf.at[core], m_buf.at[core], EV_M, near["core"])
    send(m_buf.at[core], m_buf.at[2 + core], EV_M + 1, near["mate"])
    send(m_buf.at[core], m_buf.at[2 + core], EV_M + 2, near["mate2"])

    load_x.wait()
    theirs = x_buf.at[pl.ds(pl.multiple_of((1 - core) * 256, 256), 256), :]
    remote(theirs, theirs, EV_X, near["core"]).wait_recv()
    landing = w_buf.at[other + 1 - side]
    remote(landing, landing, EV_XH + 1, near["xh"]).wait_recv()

    def project(zz, first=False):
        zz = zz % 8
        weights = w_buf[pl.ds(zz * 4, 4)].reshape(512, 512)
        rows = x_buf[:, pl.ds(pl.multiple_of(zz * 512, 512), 512)]
        term = jnp.dot(rows, weights, preferred_element_type=F32)
        if first:
            sums[...] = term
        else:
            sums[...] += term

    project(z, True)

    def plane_wait(distance):
        for ring in range(2):
            source = z - distance if ring == 0 else z + distance
            for flip in range(2):
                way = ROUTE[ring, distance, flip]
                ref = w_buf.at[piece(source + 8, flip, 1 - side), part(distance, ring), :]
                remote(ref, ref, EV_P + event(ring, distance, flip), near[way]).wait_recv()

    for distance in range(1, 5):
        for flip in range(2):
            for ring in range(2):
                source = z - distance if ring == 0 else z + distance
                ref = w_buf.at[piece(source + 8, flip, side), part(distance, ring), :]
                number = event(ring, distance, flip)
                remote(ref, ref, EV_Z + number, near["z-" if ring == 0 else "z+"]).wait_recv()
                if distance < 4:
                    ring_send(ring, distance + 1, flip)
                way = ROUTE[ring, distance, flip]
                if way != "xh":
                    send(ref, ref, EV_P + number, near[way])
                elif flip == 1:
                    for mine in range(2):
                        ref = w_buf.at[piece(source + 8, 1 - mine, side), part(distance, ring), :]
                        send(ref, ref, EV_P + event(ring, distance, mine), near["xh"])
        if distance == 1:
            send(q_at(2 * core + 1 - role), q_buf.at[2 + core], EV_Q + 1, near["mate"])
            send(q_at(2 * (1 - core) + 1 - role), q_buf.at[2 + core], EV_Q + 2, near["mate2"])
        else:
            plane_wait(distance - 1)
            project(z + 8 - distance + 1)
            project(z + distance - 1)
    plane_wait(4)
    project(z + 4)

    def rotate(rows, pair, first, count):
        turned = pltpu.roll(rows, 64, 1)
        span = pl.ds(first, count)
        return rows * tables[pair * 2, span, :] + turned * tables[pair * 2 + 1, span, :]

    for kind in range(2):
        keys = sums[pl.ds(0, 512), pl.ds(kind * 128, 128)]
        k_own[kind] = rotate(keys, 0, 0, 512).astype(BF16)
        v_own[kind] = sums[pl.ds(0, 512), pl.ds(256 + kind * 128, 128)].astype(BF16)

    def kv_rows(where):
        return pl.ds(pl.multiple_of(where * 512, 512), 512)

    def k_at(where):
        return k_all.at[kv_rows(where), :]

    def v_at(where):
        return v_all.at[kv_rows(where), pl.ds(0, 128)]

    beside = y * 2 + 1 - xl

    def seen(dy, source_y):
        return jnp.logical_not((source_y == 3) & ((dy == 2) | (dy == 3)))

    def hop(dy):
        return at(y + dy, xl, core)

    send(v_own.at[1 - role], v_relay, EV_V, near["xl"])
    send(k_own.at[role], k_at(chip), EV_K + 1, near["xl"])
    send(v_own.at[role], v_at(chip), EV_V + 1, near["xl"])

    def first_hop(dy, values):
        kind = (role + dy) % 2
        if values:
            return remote(v_own.at[kind], v_at(chip), EV_V + dy * 2, hop(dy))
        return remote(k_own.at[kind], k_at(chip), EV_K + dy * 2, hop(dy))

    def second_hop_v(dy):
        source = v_at(beside) if dy == 2 else v_relay
        return remote(source, v_at(beside), EV_V + dy * 2 + 1, hop(dy))

    def second_hop_k(dy):
        rows = k_at((y + 4 - dy) % 4 * 2 + xl)
        return remote(rows, rows, EV_K + dy * 2 + 1, near["xl"])

    for values in range(2):
        for dy in (1, 3, 2):
            @pl.when(seen(dy, y))
            def _():
                first_hop(dy, values).start()

    k_all[kv_rows(chip), :] = k_own[role]
    v_all[kv_rows(chip), pl.ds(0, 128)] = v_own[role]

    load_q.wait()
    for number, slot, device in (
        (EV_Q, 1 - core, near["core"]),
        (EV_Q + 1, 2 + core, near["mate"]),
        (EV_Q + 2, 3 - core, near["mate2"]),
    ):
        remote(q_buf.at[slot], q_buf.at[slot], number, device).wait_recv()
        mark = number - EV_Q + EV_M
        remote(m_buf.at[slot], m_buf.at[slot], mark, device).wait_recv()

    mask_key = sums[pl.ds(512, 16), pl.ds(pl.multiple_of(role * 128, 128), 128)]
    mask_value = sums[pl.ds(512, 16), pl.ds(pl.multiple_of(256 + role * 128, 128), 128)]
    mask_key = jnp.broadcast_to(mask_key[0:1, :], (256, 128))
    mask_value = jnp.broadcast_to(mask_value[0:1, :], (256, 128)).astype(BF16).astype(F32)

    def build(pair):
        where = mate if pair else chip
        for i in range(2):
            slot = pair * 2 + i
            base = 4096 + slot * 512
            block = pl.ds(pl.multiple_of(where * 512 + i * 256, 256), 256)
            masked = m_buf[slot].astype(F32) > 0.5
            noisy_k = jnp.where(
                masked, rotate(mask_key, pair, i * 256, 256), k_all[block, :].astype(F32)
            ).astype(BF16)
            noisy_v = jnp.where(
                masked, mask_value, v_all[block, pl.ds(0, 128)].astype(F32)
            ).astype(BF16)
            noisy = pl.ds(base + i * 256, 256)
            k_all[noisy, :] = noisy_k
            v_all[noisy, pl.ds(0, 128)] = noisy_v
            if i == 0:
                k_all[pl.ds(base + 256, 256), :] = noisy_k
                v_all[pl.ds(base + 256, 256), :] = jnp.zeros((256, 256), BF16)
            else:
                before = pl.ds(pl.multiple_of(where * 512, 512), 256)
                k_all[pl.ds(base, 256), :] = k_all[before, :]
                v_all[pl.ds(base, 256), pl.ds(0, 128)] = v_all[before, pl.ds(0, 128)]

    def absorb(slot, start):
        span = pl.ds(pl.multiple_of(start, 512), 512)
        for tile in range(8):
            query = q_buf[slot, pl.ds(tile % 2 * 128, 128), pl.ds(tile // 2 * 128, 128)]
            scores = lax.dot_general(query, k_all[span, :], NT, preferred_element_type=F32)
            before = row_max[slot * 8 + tile]
            after = jnp.maximum(before, jnp.max(scores, 1, keepdims=True))
            shrink = jnp.exp2((before - after) * SCORE_SCALE)
            probs = jnp.exp2((scores - jnp.tile(after, (1, 4))) * SCORE_SCALE).astype(BF16)
            term = jnp.dot(probs, v_all[span, :], preferred_element_type=F32)
            total = mix[slot * 8 + tile]
            mix[slot * 8 + tile] = total * jnp.tile(shrink, (1, 2)) + term
            row_max[slot * 8 + tile] = after

    def finish(slot):
        for tile in range(8):
            total = mix[slot * 8 + tile]
            o_buf[slot, pl.ds(tile % 2 * 128, 128), pl.ds(tile // 2 * 128, 128)] = (
                total[:, :128] / total[:, 128:]
            ).astype(BF16)

    out_cols = pl.ds(pl.multiple_of(head * 512, 512), 512)

    def mate_out(i):
        number = EV_O + (i - core + 2) % 2
        return remote(o_buf.at[2 + i], out.at[:, out_cols], number, at(3 - y, xl, i))

    late = (y == 0) | (y == 2)

    def visit(number, carry):
        turn = number % 8
        first = number < 8
        dy = jnp.where(turn < 2, 0, jnp.where(turn >= 6, 2, jnp.where(turn % 2 == 0, 1, 3)))
        dx = jnp.where((turn == 1) | (turn == 4) | (turn == 5) | (turn == 7), 1, 0)
        source_y = (y + 4 - dy) % 4
        source = source_y * 2 + jnp.where(dx == 0, xl, 1 - xl)
        here = seen(dy, source_y)
        device = near["xl"]

        @pl.when(number == 1)
        def _():
            remote(v_relay, v_relay, EV_V, device).wait_recv()
            for hop_y in (1, 3):
                @pl.when(seen(hop_y, y))
                def _():
                    second_hop_v(hop_y).start()
            remote(v_at(beside), v_at(beside), EV_V + 1, device).wait_recv()

            @pl.when(seen(2, y))
            def _():
                second_hop_v(2).start()

        for hop_y, when in ((1, 2), (3, 2), (2, 4)):
            @pl.when((number == when) & seen(hop_y, (y + 4 - hop_y) % 4))
            def _():
                rows = k_at((y + 4 - hop_y) % 4 * 2 + xl)
                remote(rows, rows, EV_K + hop_y * 2, device).wait_recv()
                second_hop_k(hop_y).start()

        @pl.when(first & here & (dx == 1))
        def _():
            remote(k_at(source), k_at(source), EV_K + dy * 2 + 1, device).wait_recv()

        @pl.when(first & here & (turn > 1))
        def _():
            remote(v_at(source), v_at(source), EV_V + dy * 2 + dx, device).wait_recv()

        @pl.when(number == 0)
        def _():
            build(0)

        @pl.when(first & (source == mate))
        def _():
            build(1)

        def item(slot, carry):
            slot = (slot + 2) % 4
            other_pair = slot >= 2
            level = jnp.where(other_pair, mate, chip)
            turn_now = jnp.where(other_pair | (y >= 2), first, jnp.logical_not(first))

            @pl.when(turn_now & (source <= level))
            def _():
                absorb(slot, jnp.where(source == level, 4096 + slot * 512, source * 512))

            return carry

        lax.fori_loop(0, 4, item, 0)

        @pl.when(number == jnp.where(late, 7, 5))
        def _():
            for i in range(2):
                finish(2 + i)
                mate_out(i).start()

        return carry

    lax.fori_loop(0, jnp.where(y < 2, 16, 8), visit, 0)
    for i in range(2):
        finish(i)
    send(o_buf.at[1 - core], out.at[:, out_cols], EV_O + 2, near["core"])
    store = local(o_buf.at[core], out.at[:, out_cols], 5)
    store.wait()

    def o_at(kv_head):
        return out.at[:, pl.ds(pl.multiple_of(kv_head * 512, 512), 512)]

    for number, kv_head, device in (
        (EV_O, 2 * core + 1 - role, near["mate"]),
        (EV_O + 1, 2 * (1 - core) + 1 - role, near["mate2"]),
        (EV_O + 2, 2 * (1 - core) + role, near["core"]),
    ):
        remote(o_at(kv_head), o_at(kv_head), number, device).wait_recv()
    for i in range(2):
        mate_out(i).wait_send()
    for dy in (1, 2, 3):
        @pl.when(seen(dy, y))
        def _():
            for values in range(2):
                first_hop(dy, values).wait_send()
            second_hop_v(dy).wait_send()

        @pl.when(seen(dy, (y + 4 - dy) % 4))
        def _():
            second_hop_k(dy).wait_send()
    for copy in sends:
        copy.wait_send()


def tables_of(positions):
    half = HEAD_DIM // 2
    steps = np.arange(half, dtype=np.float32) * np.float32(2.0) / np.float32(HEAD_DIM)
    frequency = (np.float32(ROPE_BASE) ** (-steps)).astype(np.float64)
    angles = positions.astype(np.float64)[:, None] * frequency[None, :]
    cosine = np.cos(angles).astype(np.float32)
    sine = np.sin(angles).astype(np.float32)
    return jnp.asarray(np.concatenate([cosine, cosine], 1)), jnp.asarray(np.concatenate([-sine, sine], 1))


def solution(mesh):
    def shards(clean_states, noise_mask, mask_embed, queries, w_key, w_value):
        _, rows, width = clean_states.shape
        cosine, sine = tables_of(np.arange(2 * rows))
        far_cosine, far_sine = tables_of(np.arange(8) * 2 * rows)
        any_ = pl.BlockSpec(memory_space=pl.ANY)
        vmem = pl.BlockSpec(memory_space=pltpu.VMEM)
        output = pl.pallas_call(
            kernel,
            out_shape=jax.ShapeDtypeStruct((256, 2048), BF16),
            in_specs=[any_, vmem, vmem, any_, any_, any_, any_, any_, vmem, vmem],
            out_specs=vmem,
            scratch_shapes=[
                pltpu.VMEM((528, 4096), BF16),
                pltpu.VMEM((32, 128, 512), BF16),
                pltpu.VMEM((528, 512), F32),
                pltpu.VMEM((2, 512, 128), BF16),
                pltpu.VMEM((2, 512, 128), BF16),
                pltpu.VMEM((512, 128), BF16),
                pltpu.VMEM((6144, 128), BF16),
                pltpu.VMEM((6144, 256), BF16),
                pltpu.VMEM((4, 256, 512), BF16),
                pltpu.VMEM((4, 256, 128), BF16),
                pltpu.VMEM((4, 256, 512), BF16),
                pltpu.VMEM((4, 512, 128), F32),
                pltpu.VMEM((32, 128, 128), F32),
                pltpu.VMEM((32, 128, 256), F32),
                pltpu.SemaphoreType.DMA((EV_COUNT,)),
                pltpu.SemaphoreType.DMA((EV_COUNT,)),
                pltpu.SemaphoreType.DMA((10,)),
            ],
            compiler_params=pltpu.CompilerParams(
                collective_id=0, has_side_effects=True, vmem_limit_bytes=56 << 20
            ),
        )(
            clean_states[0], noise_mask, mask_embed.reshape(32, 128), queries[0],
            w_key, w_value, cosine, sine, far_cosine, far_sine,
        )
        return output[None]

    placed = (
        P("fsdp", "seq", None),
        P("fsdp", "seq"),
        P(),
        P("fsdp", "seq", None),
        P("fsdp", None),
        P("fsdp", None),
    )
    return jax.shard_map(
        shards, mesh=mesh, in_specs=placed, out_specs=P("fsdp", "seq", None), check_vma=False
    )
```

```python
import jax
import jax.numpy as jnp
import numpy as np
from jax import lax
from jax.experimental import pallas as pl
from jax.experimental.pallas import tpu as pltpu
from jax.sharding import PartitionSpec as P

MESH = pl.DeviceIdType.MESH
BF16 = jnp.bfloat16
F32 = jnp.float32
HEAD_DIM = 128
BLOCK = 256
ROPE_BASE = 500000.0
SCORE_SCALE = float(HEAD_DIM**-0.5 * np.log2(np.e))
NT = (((1,), (1,)), ((), ()))

ROUTE = {
    (0, 1, 0): "buddy", (0, 1, 1): "xl", (1, 1, 0): "buddy", (1, 1, 1): "xl",
    (0, 2, 0): "buddy", (0, 2, 1): "xl", (1, 2, 0): "xh", (1, 2, 1): "xh",
    (0, 3, 0): "buddy", (0, 3, 1): "xl", (1, 3, 0): "mate", (1, 3, 1): "xl",
    (0, 4, 0): "buddy", (0, 4, 1): "xl", (1, 4, 0): "mate", (1, 4, 1): "buddy",
}
PLANE = ((0, 1), (1, 0), (3, 0), (1, 1), (3, 1), (2, 0), (2, 1))

EV_X, EV_XH, EV_Z, EV_P = 0, 1, 3, 19
EV_Q, EV_M, EV_K, EV_V, EV_O = 35, 38, 41, 49, 57
EV_COUNT = 60


def event(ring, distance, other):
    return (ring * 4 + distance - 1) * 2 + other


def kernel(
    states, marks, mask_row, queries, w_key, w_value, cosine, sine, far_cosine, far_sine, out,
    x_buf, w_buf, sums, k_own, v_own, v_relay, k_all, v_all, q_buf, m_buf, o_buf,
    tables, row_max, mix, send_sem, recv_sem, local_sem,
):
    seq = lax.axis_index("seq")
    fsdp = lax.axis_index("fsdp")
    core = seq % 2
    chip = seq // 2
    xl = chip % 2
    y = chip // 2
    z = fsdp // 2
    xh = fsdp % 2
    role = y % 2
    side = (y + xl) % 2
    mate = (3 - y) * 2 + xl

    def at(yy, xx, cc):
        return ((yy % 4 * 2 + xx) * 2 + cc, fsdp)

    near = {
        "buddy": at(y // 2 * 2 + 1 - y % 2, xl, core),
        "xl": at(y, 1 - xl, core),
        "xh": (at(y, 1 - xl, core)[0], z * 2 + 1 - xh),
        "z+": (seq, (z + 1) % 8 * 2 + xh),
        "z-": (seq, (z + 7) % 8 * 2 + xh),
        "core": at(y, xl, 1 - core),
        "mate": at(3 - y, xl, core),
        "mate2": at(3 - y, xl, 1 - core),
    }

    def remote(src, dst, number, device):
        return pltpu.make_async_remote_copy(
            src, dst, send_sem.at[number], recv_sem.at[number],
            device_id=device, device_id_type=MESH,
        )

    locals_ = []

    def local(src, dst, number):
        copy = pltpu.make_async_copy(src, dst, local_sem.at[number])
        copy.start()
        return copy

    wide = pl.ds(pl.multiple_of(core * 256, 256), 256)
    own = fsdp * 2
    load_w = []
    for half in range(2):
        rows = pl.ds(half * 128, 128)
        load_w.append(local(w_key.at[rows, wide], w_buf.at[own + half, :, pl.ds(0, 256)], half * 2))
        load_w.append(local(w_value.at[rows, wide], w_buf.at[own + half, :, pl.ds(256, 256)], half * 2 + 1))
    my_rows = pl.ds(pl.multiple_of(core * 256, 256), 256)
    load_x = local(states, x_buf.at[my_rows, :], 4)
    head = 2 * core + role
    q_cols = pl.ds(pl.multiple_of(head * 512, 512), 512)
    load_q = local(queries.at[:, q_cols], q_buf.at[core], 5)
    load_t = []
    for number, table in enumerate((cosine, sine)):
        load_t.append(local(table, tables.at[number], 6 + number))

    peers = [at(y + dy, xl if dx == 0 else 1 - xl, core) for dy, dx in PLANE]
    peers += [near["core"], near["mate2"], near["xh"], near["z+"], near["z-"]]
    barrier = pltpu.get_barrier_semaphore()
    for peer in peers:
        pl.semaphore_signal(barrier, inc=1, device_id=peer, device_id_type=MESH)
    pl.semaphore_wait(barrier, len(peers))

    sends = []

    def send(src, dst, number, device):
        copy = remote(src, dst, number, device)
        copy.start()
        sends.append(copy)

    for copy in load_w:
        copy.wait()
    other = (z * 2 + 1 - xh) * 2

    def piece(zz, flip, half):
        aa = 1 - xh if flip else xh
        return (zz % 8 * 2 + aa) * 2 + half

    def part(distance, ring):
        if distance < 4:
            return pl.ds(0, 128)
        return pl.ds(ring * 64, 64)

    def ring_send(ring, distance, flip):
        source = z - (distance - 1) if ring == 0 else z + (distance - 1)
        ref = w_buf.at[piece(source + 8, flip, side), part(distance, ring), :]
        send(ref, ref, EV_Z + event(ring, distance, flip), near["z+" if ring == 0 else "z-"])

    send(w_buf.at[own + 1 - side], w_buf.at[own + 1 - side], EV_XH, near["xh"])
    for ring in range(2):
        ring_send(ring, 1, 0)
    send(w_buf.at[own + side], w_buf.at[own + side], EV_XH + 1, near["xh"])
    send(states, x_buf.at[my_rows, :], EV_X, near["core"])

    landing = w_buf.at[other + side]
    remote(landing, landing, EV_XH, near["xh"]).wait_recv()
    for ring in range(2):
        ring_send(ring, 1, 1)

    flags = jnp.broadcast_to(marks[...].astype(F32), (128, 256))
    m_buf[core] = jnp.transpose(flags).astype(BF16)

    def q_at(kv_head):
        return queries.at[:, pl.ds(pl.multiple_of(kv_head * 512, 512), 512)]

    send(q_at(2 * (1 - core) + role), q_buf.at[core], EV_Q, near["core"])
    send(m_buf.at[core], m_buf.at[core], EV_M, near["core"])
    send(m_buf.at[core], m_buf.at[2 + core], EV_M + 1, near["mate"])
    send(m_buf.at[core], m_buf.at[2 + core], EV_M + 2, near["mate2"])

    def project(zz, first=False):
        zz = zz % 8
        weights = w_buf[pl.ds(zz * 4, 4)].reshape(512, 512)
        rows = x_buf[:, pl.ds(pl.multiple_of(zz * 512, 512), 512)]
        term = jnp.dot(rows, weights, preferred_element_type=F32)
        if first:
            sums[...] = term
        else:
            sums[...] += term

    def plane_wait(distance):
        for ring in range(2):
            source = z - distance if ring == 0 else z + distance
            for flip in range(2):
                way = ROUTE[ring, distance, flip]
                ref = w_buf.at[piece(source + 8, flip, 1 - side), part(distance, ring), :]
                remote(ref, ref, EV_P + event(ring, distance, flip), near[way]).wait_recv()

    for distance in range(1, 5):
        for flip in range(2):
            for ring in range(2):
                source = z - distance if ring == 0 else z + distance
                ref = w_buf.at[piece(source + 8, flip, side), part(distance, ring), :]
                number = event(ring, distance, flip)
                remote(ref, ref, EV_Z + number, near["z-" if ring == 0 else "z+"]).wait_recv()
                if distance < 4:
                    ring_send(ring, distance + 1, flip)
                way = ROUTE[ring, distance, flip]
                if way != "xh":
                    send(ref, ref, EV_P + number, near[way])
                elif flip == 1:
                    for mine in range(2):
                        ref = w_buf.at[piece(source + 8, 1 - mine, side), part(distance, ring), :]
                        send(ref, ref, EV_P + event(ring, distance, mine), near["xh"])
        if distance == 1:
            mask_rows = mask_row[...].astype(F32)
            for i in range(32):
                wide_row = jnp.broadcast_to(mask_rows[i : i + 1, :], (16, 128))
                x_buf[pl.ds(512, 16), pl.ds(i * 128, 128)] = wide_row.astype(BF16)
            v_all[:, pl.ds(128, 128)] = jnp.ones((v_all.shape[0], 128), BF16)
            row_max[...] = jnp.full(row_max.shape, -1e30, F32)
            mix[...] = jnp.zeros(mix.shape, F32)

            for copy in load_t:
                copy.wait()
            near_c, near_s = tables[0], tables[1]
            for pair, where in ((1, mate), (0, chip)):
                far_c, far_s = far_cosine[pl.ds(where, 1), :], far_sine[pl.ds(where, 1), :]
                tables[pair * 2] = near_c * far_c - near_s * far_s
                tables[pair * 2 + 1] = near_s * far_c + near_c * far_s
            load_x.wait()
            theirs = x_buf.at[pl.ds(pl.multiple_of((1 - core) * 256, 256), 256), :]
            remote(theirs, theirs, EV_X, near["core"]).wait_recv()
            landing = w_buf.at[other + 1 - side]
            remote(landing, landing, EV_XH + 1, near["xh"]).wait_recv()
            project(z, True)
            send(q_at(2 * core + 1 - role), q_buf.at[2 + core], EV_Q + 1, near["mate"])
            send(q_at(2 * (1 - core) + 1 - role), q_buf.at[2 + core], EV_Q + 2, near["mate2"])
        else:
            plane_wait(distance - 1)
            project(z + 8 - distance + 1)
            project(z + distance - 1)
    plane_wait(4)
    project(z + 4)

    def rotate(rows, pair, first, count):
        turned = pltpu.roll(rows, 64, 1)
        span = pl.ds(first, count)
        return rows * tables[pair * 2, span, :] + turned * tables[pair * 2 + 1, span, :]

    for kind in range(2):
        keys = sums[pl.ds(0, 512), pl.ds(kind * 128, 128)]
        k_own[kind] = rotate(keys, 0, 0, 512).astype(BF16)
        v_own[kind] = sums[pl.ds(0, 512), pl.ds(256 + kind * 128, 128)].astype(BF16)

    def kv_rows(where):
        return pl.ds(pl.multiple_of(where * 512, 512), 512)

    def k_at(where):
        return k_all.at[kv_rows(where), :]

    def v_at(where):
        return v_all.at[kv_rows(where), pl.ds(0, 128)]

    beside = y * 2 + 1 - xl

    def seen(dy, source_y):
        return jnp.logical_not((source_y == 3) & ((dy == 2) | (dy == 3)))

    def hop(dy):
        return at(y + dy, xl, core)

    send(v_own.at[1 - role], v_relay, EV_V, near["xl"])
    send(k_own.at[role], k_at(chip), EV_K + 1, near["xl"])
    send(v_own.at[role], v_at(chip), EV_V + 1, near["xl"])

    def first_hop(dy, values):
        kind = (role + dy) % 2
        if values:
            return remote(v_own.at[kind], v_at(chip), EV_V + dy * 2, hop(dy))
        return remote(k_own.at[kind], k_at(chip), EV_K + dy * 2, hop(dy))

    def second_hop_v(dy):
        source = v_at(beside) if dy == 2 else v_relay
        return remote(source, v_at(beside), EV_V + dy * 2 + 1, hop(dy))

    def second_hop_k(dy):
        rows = k_at((y + 4 - dy) % 4 * 2 + xl)
        return remote(rows, rows, EV_K + dy * 2 + 1, near["xl"])

    for dy, values in ((1, 0), (3, 0), (1, 1), (3, 1), (2, 0), (2, 1)):
        @pl.when(seen(dy, y))
        def _():
            first_hop(dy, values).start()

    k_all[kv_rows(chip), :] = k_own[role]
    v_all[kv_rows(chip), pl.ds(0, 128)] = v_own[role]

    load_q.wait()
    for number, slot, device in (
        (EV_Q, 1 - core, near["core"]),
        (EV_Q + 1, 2 + core, near["mate"]),
        (EV_Q + 2, 3 - core, near["mate2"]),
    ):
        remote(q_buf.at[slot], q_buf.at[slot], number, device).wait_recv()
        mark = number - EV_Q + EV_M
        remote(m_buf.at[slot], m_buf.at[slot], mark, device).wait_recv()

    mask_key = sums[pl.ds(512, 16), pl.ds(pl.multiple_of(role * 128, 128), 128)]
    mask_value = sums[pl.ds(512, 16), pl.ds(pl.multiple_of(256 + role * 128, 128), 128)]
    mask_key = jnp.broadcast_to(mask_key[0:1, :], (256, 128))
    mask_value = jnp.broadcast_to(mask_value[0:1, :], (256, 128)).astype(BF16).astype(F32)

    def build(pair):
        where = mate if pair else chip
        for i in range(2):
            slot = pair * 2 + i
            base = 4096 + slot * 512
            block = pl.ds(pl.multiple_of(where * 512 + i * 256, 256), 256)
            masked = m_buf[slot].astype(F32) > 0.5
            noisy_k = jnp.where(
                masked, rotate(mask_key, pair, i * 256, 256), k_all[block, :].astype(F32)
            ).astype(BF16)
            noisy_v = jnp.where(
                masked, mask_value, v_all[block, pl.ds(0, 128)].astype(F32)
            ).astype(BF16)
            noisy = pl.ds(base + i * 256, 256)
            k_all[noisy, :] = noisy_k
            v_all[noisy, pl.ds(0, 128)] = noisy_v
            if i == 0:
                k_all[pl.ds(base + 256, 256), :] = noisy_k
                v_all[pl.ds(base + 256, 256), :] = jnp.zeros((256, 256), BF16)
            else:
                before = pl.ds(pl.multiple_of(where * 512, 512), 256)
                k_all[pl.ds(base, 256), :] = k_all[before, :]
                v_all[pl.ds(base, 256), pl.ds(0, 128)] = v_all[before, pl.ds(0, 128)]

    def absorb(slot, start):
        span = pl.ds(pl.multiple_of(start, 512), 512)
        for tile in range(8):
            query = q_buf[slot, pl.ds(tile % 2 * 128, 128), pl.ds(tile // 2 * 128, 128)]
            scores = lax.dot_general(query, k_all[span, :], NT, preferred_element_type=F32)
            before = row_max[slot * 8 + tile]
            after = jnp.maximum(before, jnp.max(scores, 1, keepdims=True))
            shrink = jnp.exp2((before - after) * SCORE_SCALE)
            probs = jnp.exp2((scores - jnp.tile(after, (1, 4))) * SCORE_SCALE).astype(BF16)
            term = jnp.dot(probs, v_all[span, :], preferred_element_type=F32)
            total = mix[slot * 8 + tile]
            mix[slot * 8 + tile] = total * jnp.tile(shrink, (1, 2)) + term
            row_max[slot * 8 + tile] = after

    def finish(slot):
        for tile in range(8):
            total = mix[slot * 8 + tile]
            o_buf[slot, pl.ds(tile % 2 * 128, 128), pl.ds(tile // 2 * 128, 128)] = (
                total[:, :128] / total[:, 128:]
            ).astype(BF16)

    out_cols = pl.ds(pl.multiple_of(head * 512, 512), 512)

    def mate_out(i):
        number = EV_O + (i - core + 2) % 2
        return remote(o_buf.at[2 + i], out.at[:, out_cols], number, at(3 - y, xl, i))

    late = (y == 0) | (y == 2)

    def source_of(turn):
        dy = jnp.where(turn >= 6, 2, jnp.where((turn == 0) | (turn == 3), 0, jnp.where((turn == 1) | (turn == 4), 1, 3)))
        dx = jnp.where((turn == 3) | (turn == 4) | (turn == 5) | (turn == 7), 1, 0)
        source_y = (y + 4 - dy) % 4
        return dy, dx, source_y, source_y * 2 + jnp.where(dx == 0, xl, 1 - xl)

    def visit(number, carry):
        turn = number % 8
        first = number < 8
        dy, dx, source_y, source = source_of(turn)
        here = first & seen(dy, source_y)
        device = near["xl"]

        def pass_on_k(hop_y):
            @pl.when(seen(hop_y, (y + 4 - hop_y) % 4))
            def _():
                rows = k_at((y + 4 - hop_y) % 4 * 2 + xl)
                remote(rows, rows, EV_K + hop_y * 2, device).wait_recv()
                second_hop_k(hop_y).start()

        def pass_on_v(hop_y):
            @pl.when(seen(hop_y, y))
            def _():
                second_hop_v(hop_y).start()

        @pl.when(number == 1)
        def _():
            remote(v_relay, v_relay, EV_V, device).wait_recv()
            pass_on_v(1)
            pass_on_v(3)
            pass_on_k(1)
            pass_on_k(3)

        @pl.when(number == 3)
        def _():
            remote(v_at(beside), v_at(beside), EV_V + 1, device).wait_recv()
            pass_on_v(2)
            pass_on_k(2)

        @pl.when(here & (dx == 1))
        def _():
            remote(k_at(source), k_at(source), EV_K + dy * 2 + 1, device).wait_recv()

        @pl.when(here & (turn != 0) & (turn != 3))
        def _():
            remote(v_at(source), v_at(source), EV_V + dy * 2 + dx, device).wait_recv()

        @pl.when(number == 0)
        def _():
            build(0)

        @pl.when(first & (source == mate))
        def _():
            build(1)

        def item(index, carry):
            both = turn == 7
            slot = (jnp.where(both, index // 2, index) + 2) % 4
            _, _, _, earlier = source_of(6)
            origin = jnp.where(both & (index % 2 == 0), earlier, source)
            other_pair = slot >= 2
            level = jnp.where(other_pair, mate, chip)
            turn_now = jnp.where(other_pair | (y >= 2), first, jnp.logical_not(first))

            @pl.when(turn_now & (origin <= level))
            def _():
                absorb(slot, jnp.where(origin == level, 4096 + slot * 512, origin * 512))

            done = number == jnp.where(late, 7, 5)

            @pl.when(other_pair & done & ((turn < 7) | (index % 2 == 1)))
            def _():
                finish(slot)
                mate_out(slot - 2).start()

            return carry

        lax.fori_loop(0, jnp.where(turn < 6, 4, jnp.where(turn == 6, 0, 8)), item, 0)
        return carry

    lax.fori_loop(0, jnp.where(y < 2, 16, 8), visit, 0)
    for i in range(2):
        finish(i)
    send(o_buf.at[1 - core], out.at[:, out_cols], EV_O + 2, near["core"])
    store = local(o_buf.at[core], out.at[:, out_cols], 5)
    store.wait()

    def o_at(kv_head):
        return out.at[:, pl.ds(pl.multiple_of(kv_head * 512, 512), 512)]

    for number, kv_head, device in (
        (EV_O, 2 * core + 1 - role, near["mate"]),
        (EV_O + 1, 2 * (1 - core) + 1 - role, near["mate2"]),
        (EV_O + 2, 2 * (1 - core) + role, near["core"]),
    ):
        remote(o_at(kv_head), o_at(kv_head), number, device).wait_recv()
    for i in range(2):
        mate_out(i).wait_send()
    for dy in (1, 2, 3):
        @pl.when(seen(dy, y))
        def _():
            for values in range(2):
                first_hop(dy, values).wait_send()
            second_hop_v(dy).wait_send()

        @pl.when(seen(dy, (y + 4 - dy) % 4))
        def _():
            second_hop_k(dy).wait_send()
    for copy in sends:
        copy.wait_send()


def tables_of(positions):
    half = HEAD_DIM // 2
    steps = np.arange(half, dtype=np.float32) * np.float32(2.0) / np.float32(HEAD_DIM)
    frequency = (np.float32(ROPE_BASE) ** (-steps)).astype(np.float64)
    angles = positions.astype(np.float64)[:, None] * frequency[None, :]
    cosine = np.cos(angles).astype(np.float32)
    sine = np.sin(angles).astype(np.float32)
    return jnp.asarray(np.concatenate([cosine, cosine], 1)), jnp.asarray(np.concatenate([-sine, sine], 1))


def solution(mesh):
    def shards(clean_states, noise_mask, mask_embed, queries, w_key, w_value):
        _, rows, width = clean_states.shape
        cosine, sine = tables_of(np.arange(2 * rows))
        far_cosine, far_sine = tables_of(np.arange(8) * 2 * rows)
        any_ = pl.BlockSpec(memory_space=pl.ANY)
        vmem = pl.BlockSpec(memory_space=pltpu.VMEM)
        output = pl.pallas_call(
            kernel,
            out_shape=jax.ShapeDtypeStruct((256, 2048), BF16),
            in_specs=[any_, vmem, vmem, any_, any_, any_, any_, any_, vmem, vmem],
            out_specs=vmem,
            scratch_shapes=[
                pltpu.VMEM((528, 4096), BF16),
                pltpu.VMEM((32, 128, 512), BF16),
                pltpu.VMEM((528, 512), F32),
                pltpu.VMEM((2, 512, 128), BF16),
                pltpu.VMEM((2, 512, 128), BF16),
                pltpu.VMEM((512, 128), BF16),
                pltpu.VMEM((6144, 128), BF16),
                pltpu.VMEM((6144, 256), BF16),
                pltpu.VMEM((4, 256, 512), BF16),
                pltpu.VMEM((4, 256, 128), BF16),
                pltpu.VMEM((4, 256, 512), BF16),
                pltpu.VMEM((4, 512, 128), F32),
                pltpu.VMEM((32, 128, 128), F32),
                pltpu.VMEM((32, 128, 256), F32),
                pltpu.SemaphoreType.DMA((EV_COUNT,)),
                pltpu.SemaphoreType.DMA((EV_COUNT,)),
                pltpu.SemaphoreType.DMA((10,)),
            ],
            compiler_params=pltpu.CompilerParams(
                collective_id=0, has_side_effects=True, vmem_limit_bytes=56 << 20
            ),
        )(
            clean_states[0], noise_mask, mask_embed.reshape(32, 128), queries[0],
            w_key, w_value, cosine, sine, far_cosine, far_sine,
        )
        return output[None]

    placed = (
        P("fsdp", "seq", None),
        P("fsdp", "seq"),
        P(),
        P("fsdp", "seq", None),
        P("fsdp", None),
        P("fsdp", None),
    )
    return jax.shard_map(
        shards, mesh=mesh, in_specs=placed, out_specs=P("fsdp", "seq", None), check_vma=False
    )
```

```python
import jax
import jax.numpy as jnp
import numpy as np
from jax import lax
from jax.experimental import pallas as pl
from jax.experimental.pallas import tpu as pltpu
from jax.sharding import PartitionSpec as P

MESH = pl.DeviceIdType.MESH
BF16 = jnp.bfloat16
F32 = jnp.float32
HEAD_DIM = 128
BLOCK = 256
ROPE_BASE = 500000.0
SCORE_SCALE = float(HEAD_DIM**-0.5 * np.log2(np.e))
NT = (((1,), (1,)), ((), ()))

ROUTE = {
    (0, 1, 0): "buddy", (0, 1, 1): "xl", (1, 1, 0): "buddy", (1, 1, 1): "xl",
    (0, 2, 0): "buddy", (0, 2, 1): "xl", (1, 2, 0): "xh", (1, 2, 1): "xh",
    (0, 3, 0): "buddy", (0, 3, 1): "xl", (1, 3, 0): "mate", (1, 3, 1): "xl",
    (0, 4, 0): "buddy", (0, 4, 1): "xl", (1, 4, 0): "mate", (1, 4, 1): "buddy",
}
PLANE = ((0, 1), (1, 0), (3, 0), (1, 1), (3, 1), (2, 0), (2, 1))

EV_X, EV_XH, EV_Z, EV_P = 0, 1, 3, 19
EV_Q, EV_M, EV_K, EV_V, EV_O = 35, 38, 41, 49, 57
EV_COUNT = 60


def event(ring, distance, other):
    return (ring * 4 + distance - 1) * 2 + other


def kernel(
    states, marks, mask_row, queries, w_key, w_value, cosine, sine, far_cosine, far_sine, out,
    x_buf, w_buf, sums, k_own, v_own, v_relay, k_all, v_all, q_buf, m_buf, o_buf,
    tables, row_max, mix, send_sem, recv_sem, local_sem,
):
    seq = lax.axis_index("seq")
    fsdp = lax.axis_index("fsdp")
    core = seq % 2
    chip = seq // 2
    xl = chip % 2
    y = chip // 2
    z = fsdp // 2
    xh = fsdp % 2
    role = y % 2
    side = (y + xl) % 2
    mate = (3 - y) * 2 + xl

    def at(yy, xx, cc):
        return ((yy % 4 * 2 + xx) * 2 + cc, fsdp)

    near = {
        "buddy": at(y // 2 * 2 + 1 - y % 2, xl, core),
        "xl": at(y, 1 - xl, core),
        "xh": (at(y, 1 - xl, core)[0], z * 2 + 1 - xh),
        "z+": (seq, (z + 1) % 8 * 2 + xh),
        "z-": (seq, (z + 7) % 8 * 2 + xh),
        "core": at(y, xl, 1 - core),
        "mate": at(3 - y, xl, core),
        "mate2": at(3 - y, xl, 1 - core),
    }

    def remote(src, dst, number, device):
        return pltpu.make_async_remote_copy(
            src, dst, send_sem.at[number], recv_sem.at[number],
            device_id=device, device_id_type=MESH,
        )

    locals_ = []

    def local(src, dst, number):
        copy = pltpu.make_async_copy(src, dst, local_sem.at[number])
        copy.start()
        return copy

    wide = pl.ds(pl.multiple_of(core * 256, 256), 256)
    own = fsdp * 2
    load_w = []
    for half in range(2):
        rows = pl.ds(half * 128, 128)
        load_w.append(local(w_key.at[rows, wide], w_buf.at[own + half, :, pl.ds(0, 256)], half * 2))
        load_w.append(local(w_value.at[rows, wide], w_buf.at[own + half, :, pl.ds(256, 256)], half * 2 + 1))
    my_rows = pl.ds(pl.multiple_of(core * 256, 256), 256)
    load_x = local(states, x_buf.at[my_rows, :], 4)
    head = 2 * core + role
    q_cols = pl.ds(pl.multiple_of(head * 512, 512), 512)
    load_q = local(queries.at[:, q_cols], q_buf.at[core], 5)
    load_t = []
    for number, table in enumerate((cosine, sine)):
        load_t.append(local(table, tables.at[number], 6 + number))

    peers = [at(y + dy, xl if dx == 0 else 1 - xl, core) for dy, dx in PLANE]
    peers += [near["core"], near["mate2"], near["xh"], near["z+"], near["z-"]]
    barrier = pltpu.get_barrier_semaphore()
    for peer in peers:
        pl.semaphore_signal(barrier, inc=1, device_id=peer, device_id_type=MESH)
    pl.semaphore_wait(barrier, len(peers))

    sends = []

    def send(src, dst, number, device):
        copy = remote(src, dst, number, device)
        copy.start()
        sends.append(copy)

    for copy in load_w:
        copy.wait()
    other = (z * 2 + 1 - xh) * 2

    def piece(zz, flip, half):
        aa = 1 - xh if flip else xh
        return (zz % 8 * 2 + aa) * 2 + half

    def part(distance, ring):
        if distance < 4:
            return pl.ds(0, 128)
        return pl.ds(ring * 64, 64)

    def ring_send(ring, distance, flip):
        source = z - (distance - 1) if ring == 0 else z + (distance - 1)
        ref = w_buf.at[piece(source + 8, flip, side), part(distance, ring), :]
        send(ref, ref, EV_Z + event(ring, distance, flip), near["z+" if ring == 0 else "z-"])

    send(w_buf.at[own + 1 - side], w_buf.at[own + 1 - side], EV_XH, near["xh"])
    for ring in range(2):
        ring_send(ring, 1, 0)
    send(w_buf.at[own + side], w_buf.at[own + side], EV_XH + 1, near["xh"])
    send(states, x_buf.at[my_rows, :], EV_X, near["core"])

    landing = w_buf.at[other + side]
    remote(landing, landing, EV_XH, near["xh"]).wait_recv()
    for ring in range(2):
        ring_send(ring, 1, 1)

    flags = jnp.broadcast_to(marks[...].astype(F32), (128, 256))
    m_buf[core] = jnp.transpose(flags).astype(BF16)

    def q_at(kv_head):
        return queries.at[:, pl.ds(pl.multiple_of(kv_head * 512, 512), 512)]

    send(q_at(2 * (1 - core) + role), q_buf.at[core], EV_Q, near["core"])
    send(m_buf.at[core], m_buf.at[core], EV_M, near["core"])
    send(m_buf.at[core], m_buf.at[2 + core], EV_M + 1, near["mate"])
    send(m_buf.at[core], m_buf.at[2 + core], EV_M + 2, near["mate2"])

    def project(zz, first=False):
        zz = zz % 8
        weights = w_buf[pl.ds(zz * 4, 4)].reshape(512, 512)
        rows = x_buf[:, pl.ds(pl.multiple_of(zz * 512, 512), 512)]
        term = jnp.dot(rows, weights, preferred_element_type=F32)
        if first:
            sums[...] = term
        else:
            sums[...] += term

    def plane_wait(distance):
        for ring in range(2):
            source = z - distance if ring == 0 else z + distance
            for flip in range(2):
                way = ROUTE[ring, distance, flip]
                ref = w_buf.at[piece(source + 8, flip, 1 - side), part(distance, ring), :]
                remote(ref, ref, EV_P + event(ring, distance, flip), near[way]).wait_recv()

    for distance in range(1, 5):
        for flip in range(2):
            for ring in range(2):
                source = z - distance if ring == 0 else z + distance
                ref = w_buf.at[piece(source + 8, flip, side), part(distance, ring), :]
                number = event(ring, distance, flip)
                remote(ref, ref, EV_Z + number, near["z-" if ring == 0 else "z+"]).wait_recv()
                if distance < 4:
                    ring_send(ring, distance + 1, flip)
                way = ROUTE[ring, distance, flip]
                if way != "xh":
                    send(ref, ref, EV_P + number, near[way])
                elif flip == 1:
                    for mine in range(2):
                        ref = w_buf.at[piece(source + 8, 1 - mine, side), part(distance, ring), :]
                        send(ref, ref, EV_P + event(ring, distance, mine), near["xh"])
        if distance == 1:
            mask_rows = mask_row[...].astype(F32)
            for i in range(32):
                wide_row = jnp.broadcast_to(mask_rows[i : i + 1, :], (16, 128))
                x_buf[pl.ds(512, 16), pl.ds(i * 128, 128)] = wide_row.astype(BF16)
            v_all[:, pl.ds(128, 128)] = jnp.ones((v_all.shape[0], 128), BF16)
            row_max[...] = jnp.full(row_max.shape, -1e30, F32)
            mix[...] = jnp.zeros(mix.shape, F32)

            for copy in load_t:
                copy.wait()
            near_c, near_s = tables[0], tables[1]
            for pair, where in ((1, mate), (0, chip)):
                far_c, far_s = far_cosine[pl.ds(where, 1), :], far_sine[pl.ds(where, 1), :]
                tables[pair * 2] = near_c * far_c - near_s * far_s
                tables[pair * 2 + 1] = near_s * far_c + near_c * far_s
            load_x.wait()
            theirs = x_buf.at[pl.ds(pl.multiple_of((1 - core) * 256, 256), 256), :]
            remote(theirs, theirs, EV_X, near["core"]).wait_recv()
            landing = w_buf.at[other + 1 - side]
            remote(landing, landing, EV_XH + 1, near["xh"]).wait_recv()
            project(z, True)
            send(q_at(2 * core + 1 - role), q_buf.at[2 + core], EV_Q + 1, near["mate"])
            send(q_at(2 * (1 - core) + 1 - role), q_buf.at[2 + core], EV_Q + 2, near["mate2"])
        else:
            plane_wait(distance - 1)
            project(z + 8 - distance + 1)
            project(z + distance - 1)
    plane_wait(4)
    project(z + 4)

    def rotate(rows, pair, first, count):
        turned = pltpu.roll(rows, 64, 1)
        span = pl.ds(first, count)
        return rows * tables[pair * 2, span, :] + turned * tables[pair * 2 + 1, span, :]

    for kind in range(2):
        keys = sums[pl.ds(0, 512), pl.ds(kind * 128, 128)]
        k_own[kind] = rotate(keys, 0, 0, 512).astype(BF16)
        v_own[kind] = sums[pl.ds(0, 512), pl.ds(256 + kind * 128, 128)].astype(BF16)

    def kv_rows(where):
        return pl.ds(pl.multiple_of(where * 512, 512), 512)

    def k_at(where):
        return k_all.at[kv_rows(where), :]

    def v_at(where):
        return v_all.at[kv_rows(where), pl.ds(0, 128)]

    beside = y * 2 + 1 - xl

    def seen(dy, source_y):
        return jnp.logical_not((source_y == 3) & ((dy == 2) | (dy == 3)))

    def hop(dy):
        return at(y + dy, xl, core)

    send(v_own.at[1 - role], v_relay, EV_V, near["xl"])
    send(k_own.at[role], k_at(chip), EV_K + 1, near["xl"])
    send(v_own.at[role], v_at(chip), EV_V + 1, near["xl"])

    def first_hop(dy, values):
        kind = (role + dy) % 2
        if values:
            return remote(v_own.at[kind], v_at(chip), EV_V + dy * 2, hop(dy))
        return remote(k_own.at[kind], k_at(chip), EV_K + dy * 2, hop(dy))

    def second_hop_v(dy):
        source = v_at(beside) if dy == 2 else v_relay
        return remote(source, v_at(beside), EV_V + dy * 2 + 1, hop(dy))

    def second_hop_k(dy):
        rows = k_at((y + 4 - dy) % 4 * 2 + xl)
        return remote(rows, rows, EV_K + dy * 2 + 1, near["xl"])

    for dy, values in ((1, 0), (3, 0), (1, 1), (3, 1), (2, 0), (2, 1)):
        @pl.when(seen(dy, y))
        def _():
            first_hop(dy, values).start()

    k_all[kv_rows(chip), :] = k_own[role]
    v_all[kv_rows(chip), pl.ds(0, 128)] = v_own[role]

    load_q.wait()
    for number, slot, device in (
        (EV_Q, 1 - core, near["core"]),
        (EV_Q + 1, 2 + core, near["mate"]),
        (EV_Q + 2, 3 - core, near["mate2"]),
    ):
        remote(q_buf.at[slot], q_buf.at[slot], number, device).wait_recv()
        mark = number - EV_Q + EV_M
        remote(m_buf.at[slot], m_buf.at[slot], mark, device).wait_recv()

    mask_key = sums[pl.ds(512, 16), pl.ds(pl.multiple_of(role * 128, 128), 128)]
    mask_value = sums[pl.ds(512, 16), pl.ds(pl.multiple_of(256 + role * 128, 128), 128)]
    mask_key = jnp.broadcast_to(mask_key[0:1, :], (256, 128))
    mask_value = jnp.broadcast_to(mask_value[0:1, :], (256, 128)).astype(BF16).astype(F32)

    def build(pair):
        where = mate if pair else chip
        for i in range(2):
            slot = pair * 2 + i
            base = 4096 + slot * 512
            block = pl.ds(pl.multiple_of(where * 512 + i * 256, 256), 256)
            masked = m_buf[slot].astype(F32) > 0.5
            noisy_k = jnp.where(
                masked, rotate(mask_key, pair, i * 256, 256), k_all[block, :].astype(F32)
            ).astype(BF16)
            noisy_v = jnp.where(
                masked, mask_value, v_all[block, pl.ds(0, 128)].astype(F32)
            ).astype(BF16)
            noisy = pl.ds(base + i * 256, 256)
            k_all[noisy, :] = noisy_k
            v_all[noisy, pl.ds(0, 128)] = noisy_v
            if i == 0:
                k_all[pl.ds(base + 256, 256), :] = noisy_k
                v_all[pl.ds(base + 256, 256), :] = jnp.zeros((256, 256), BF16)
            else:
                before = pl.ds(pl.multiple_of(where * 512, 512), 256)
                k_all[pl.ds(base, 256), :] = k_all[before, :]
                v_all[pl.ds(base, 256), pl.ds(0, 128)] = v_all[before, pl.ds(0, 128)]

    def absorb(slot, start):
        span = pl.ds(pl.multiple_of(start, 512), 512)
        for tile in range(8):
            query = q_buf[slot, pl.ds(tile % 2 * 128, 128), pl.ds(tile // 2 * 128, 128)]
            scores = lax.dot_general(query, k_all[span, :], NT, preferred_element_type=F32)
            before = row_max[slot * 8 + tile]
            after = jnp.maximum(before, jnp.max(scores, 1, keepdims=True))
            shrink = jnp.exp2((before - after) * SCORE_SCALE)
            probs = jnp.exp2((scores - jnp.tile(after, (1, 4))) * SCORE_SCALE).astype(BF16)
            term = jnp.dot(probs, v_all[span, :], preferred_element_type=F32)
            total = mix[slot * 8 + tile]
            mix[slot * 8 + tile] = total * jnp.tile(shrink, (1, 2)) + term
            row_max[slot * 8 + tile] = after

    def finish(slot):
        for tile in range(8):
            total = mix[slot * 8 + tile]
            o_buf[slot, pl.ds(tile % 2 * 128, 128), pl.ds(tile // 2 * 128, 128)] = (
                total[:, :128] / total[:, 128:]
            ).astype(BF16)

    out_cols = pl.ds(pl.multiple_of(head * 512, 512), 512)

    def mate_out(i):
        number = EV_O + (i - core + 2) % 2
        return remote(o_buf.at[2 + i], out.at[:, out_cols], number, at(3 - y, xl, i))

    late = (y == 0) | (y == 2)

    def source_of(turn):
        dy = jnp.where(turn >= 6, 2, jnp.where((turn == 0) | (turn == 3), 0, jnp.where((turn == 1) | (turn == 4), 1, 3)))
        dx = jnp.where((turn == 3) | (turn == 4) | (turn == 5) | (turn == 7), 1, 0)
        source_y = (y + 4 - dy) % 4
        return dy, dx, source_y, source_y * 2 + jnp.where(dx == 0, xl, 1 - xl)

    def visit(number, carry):
        turn = number % 8
        first = number < 8
        dy, dx, source_y, source = source_of(turn)
        here = first & seen(dy, source_y)
        device = near["xl"]

        def pass_on_k(hop_y):
            @pl.when(seen(hop_y, (y + 4 - hop_y) % 4))
            def _():
                rows = k_at((y + 4 - hop_y) % 4 * 2 + xl)
                remote(rows, rows, EV_K + hop_y * 2, device).wait_recv()
                second_hop_k(hop_y).start()

        def pass_on_v(hop_y):
            @pl.when(seen(hop_y, y))
            def _():
                second_hop_v(hop_y).start()

        @pl.when(number == 1)
        def _():
            remote(v_relay, v_relay, EV_V, device).wait_recv()
            pass_on_v(1)
            pass_on_v(3)
            pass_on_k(1)
            pass_on_k(3)

        @pl.when(number == 3)
        def _():
            remote(v_at(beside), v_at(beside), EV_V + 1, device).wait_recv()
            pass_on_v(2)
            pass_on_k(2)

        @pl.when(here & (dx == 1))
        def _():
            remote(k_at(source), k_at(source), EV_K + dy * 2 + 1, device).wait_recv()

        @pl.when(here & (turn != 0) & (turn != 3))
        def _():
            remote(v_at(source), v_at(source), EV_V + dy * 2 + dx, device).wait_recv()

        @pl.when(number == 0)
        def _():
            build(0)

        @pl.when(first & (source == mate))
        def _():
            build(1)

        def item(index, carry):
            both = turn == 7
            slot = (jnp.where(both, index // 2, index) + 2) % 4
            _, _, _, earlier = source_of(6)
            origin = jnp.where(both & (index % 2 == 0), earlier, source)
            other_pair = slot >= 2
            level = jnp.where(other_pair, mate, chip)
            turn_now = jnp.where(other_pair | (y >= 2), first, jnp.logical_not(first))

            @pl.when(turn_now & (origin <= level))
            def _():
                absorb(slot, jnp.where(origin == level, 4096 + slot * 512, origin * 512))

            done = number == jnp.where(late, 7, 5)

            @pl.when(other_pair & done & ((turn < 7) | (index % 2 == 1)))
            def _():
                finish(slot)
                mate_out(slot - 2).start()

            return carry

        lax.fori_loop(0, jnp.where(turn < 6, 4, jnp.where(turn == 6, 0, 8)), item, 0)
        return carry

    lax.fori_loop(0, jnp.where(y < 2, 16, 8), visit, 0)
    for i in range(2):
        finish(i)
    send(o_buf.at[1 - core], out.at[:, out_cols], EV_O + 2, near["core"])
    store = local(o_buf.at[core], out.at[:, out_cols], 5)
    store.wait()

    def o_at(kv_head):
        return out.at[:, pl.ds(pl.multiple_of(kv_head * 512, 512), 512)]

    for number, kv_head, device in (
        (EV_O, 2 * core + 1 - role, near["mate"]),
        (EV_O + 1, 2 * (1 - core) + 1 - role, near["mate2"]),
        (EV_O + 2, 2 * (1 - core) + role, near["core"]),
    ):
        remote(o_at(kv_head), o_at(kv_head), number, device).wait_recv()
    for i in range(2):
        mate_out(i).wait_send()
    for dy in (1, 2, 3):
        @pl.when(seen(dy, y))
        def _():
            for values in range(2):
                first_hop(dy, values).wait_send()
            second_hop_v(dy).wait_send()

        @pl.when(seen(dy, (y + 4 - dy) % 4))
        def _():
            second_hop_k(dy).wait_send()
    for copy in sends:
        copy.wait_send()


def tables_of(positions):
    half = HEAD_DIM // 2
    steps = np.arange(half, dtype=np.float32) * np.float32(2.0) / np.float32(HEAD_DIM)
    frequency = (np.float32(ROPE_BASE) ** (-steps)).astype(np.float64)
    angles = positions.astype(np.float64)[:, None] * frequency[None, :]
    cosine = np.cos(angles).astype(np.float32)
    sine = np.sin(angles).astype(np.float32)
    return jnp.asarray(np.concatenate([cosine, cosine], 1)), jnp.asarray(np.concatenate([-sine, sine], 1))


def solution(mesh):
    def shards(clean_states, noise_mask, mask_embed, queries, w_key, w_value):
        _, rows, width = clean_states.shape
        cosine, sine = tables_of(np.arange(2 * rows))
        far_cosine, far_sine = tables_of(np.arange(8) * 2 * rows)
        any_ = pl.BlockSpec(memory_space=pl.ANY)
        vmem = pl.BlockSpec(memory_space=pltpu.VMEM)
        output = pl.pallas_call(
            kernel,
            out_shape=pltpu.VMEM((256, 2048), BF16),
            in_specs=[any_, vmem, vmem, any_, any_, any_, any_, any_, vmem, vmem],
            out_specs=vmem,
            scratch_shapes=[
                pltpu.VMEM((528, 4096), BF16),
                pltpu.VMEM((32, 128, 512), BF16),
                pltpu.VMEM((528, 512), F32),
                pltpu.VMEM((2, 512, 128), BF16),
                pltpu.VMEM((2, 512, 128), BF16),
                pltpu.VMEM((512, 128), BF16),
                pltpu.VMEM((6144, 128), BF16),
                pltpu.VMEM((6144, 256), BF16),
                pltpu.VMEM((4, 256, 512), BF16),
                pltpu.VMEM((4, 256, 128), BF16),
                pltpu.VMEM((4, 256, 512), BF16),
                pltpu.VMEM((4, 512, 128), F32),
                pltpu.VMEM((32, 128, 128), F32),
                pltpu.VMEM((32, 128, 256), F32),
                pltpu.SemaphoreType.DMA((EV_COUNT,)),
                pltpu.SemaphoreType.DMA((EV_COUNT,)),
                pltpu.SemaphoreType.DMA((10,)),
            ],
            compiler_params=pltpu.CompilerParams(
                collective_id=0, has_side_effects=True, vmem_limit_bytes=56 << 20
            ),
        )(
            clean_states[0], noise_mask, mask_embed.reshape(32, 128), queries[0],
            w_key, w_value, cosine, sine, far_cosine, far_sine,
        )
        return output[None]

    placed = (
        P("fsdp", "seq", None),
        P("fsdp", "seq"),
        P(),
        P("fsdp", "seq", None),
        P("fsdp", None),
        P("fsdp", None),
    )
    return jax.shard_map(
        shards, mesh=mesh, in_specs=placed, out_specs=P("fsdp", "seq", None), check_vma=False
    )
```

```python
import jax
import jax.numpy as jnp
import numpy as np
from jax import lax
from jax.experimental import pallas as pl
from jax.experimental.pallas import tpu as pltpu
from jax.sharding import PartitionSpec as P

MESH = pl.DeviceIdType.MESH
BF16 = jnp.bfloat16
F32 = jnp.float32
HEAD_DIM = 128
BLOCK = 256
ROPE_BASE = 500000.0
SCORE_SCALE = float(HEAD_DIM**-0.5 * np.log2(np.e))
NT = (((1,), (1,)), ((), ()))

ROUTE = {
    (0, 1, 0): "buddy", (0, 1, 1): "xl", (1, 1, 0): "buddy", (1, 1, 1): "xl",
    (0, 2, 0): "buddy", (0, 2, 1): "xl", (1, 2, 0): "xh", (1, 2, 1): "xh",
    (0, 3, 0): "buddy", (0, 3, 1): "xl", (1, 3, 0): "mate", (1, 3, 1): "xl",
    (0, 4, 0): "buddy", (0, 4, 1): "xl", (1, 4, 0): "mate", (1, 4, 1): "buddy",
}
PLANE = ((0, 1), (1, 0), (3, 0), (1, 1), (3, 1), (2, 0), (2, 1))

EV_X, EV_XH, EV_Z, EV_P = 0, 1, 3, 19
EV_Q, EV_M, EV_K, EV_V, EV_O = 35, 38, 41, 49, 57
EV_COUNT = 60


def event(ring, distance, other):
    return (ring * 4 + distance - 1) * 2 + other


def kernel(
    states, marks, mask_row, queries, w_key, w_value, cosine, sine, far_cosine, far_sine, out,
    x_buf, w_buf, sums, k_own, v_own, v_relay, k_all, v_all, q_buf, m_buf, o_buf,
    tables, row_max, mix, send_sem, recv_sem, local_sem,
):
    seq = lax.axis_index("seq")
    fsdp = lax.axis_index("fsdp")
    core = seq % 2
    chip = seq // 2
    xl = chip % 2
    y = chip // 2
    z = fsdp // 2
    xh = fsdp % 2
    role = y % 2
    side = (y + xl) % 2
    mate = (3 - y) * 2 + xl

    def at(yy, xx, cc):
        return ((yy % 4 * 2 + xx) * 2 + cc, fsdp)

    near = {
        "buddy": at(y // 2 * 2 + 1 - y % 2, xl, core),
        "xl": at(y, 1 - xl, core),
        "xh": (at(y, 1 - xl, core)[0], z * 2 + 1 - xh),
        "z+": (seq, (z + 1) % 8 * 2 + xh),
        "z-": (seq, (z + 7) % 8 * 2 + xh),
        "core": at(y, xl, 1 - core),
        "mate": at(3 - y, xl, core),
        "mate2": at(3 - y, xl, 1 - core),
    }

    def remote(src, dst, number, device):
        return pltpu.make_async_remote_copy(
            src, dst, send_sem.at[number], recv_sem.at[number],
            device_id=device, device_id_type=MESH,
        )

    locals_ = []

    def local(src, dst, number):
        copy = pltpu.make_async_copy(src, dst, local_sem.at[number])
        copy.start()
        return copy

    wide = pl.ds(pl.multiple_of(core * 256, 256), 256)
    own = fsdp * 2
    load_w = []
    for half in range(2):
        rows = pl.ds(half * 128, 128)
        load_w.append(local(w_key.at[rows, wide], w_buf.at[own + half, :, pl.ds(0, 256)], half * 2))
        load_w.append(local(w_value.at[rows, wide], w_buf.at[own + half, :, pl.ds(256, 256)], half * 2 + 1))
    my_rows = pl.ds(pl.multiple_of(core * 256, 256), 256)
    load_x = local(states, x_buf.at[my_rows, :], 4)
    head = 2 * core + role
    q_cols = pl.ds(pl.multiple_of(head * 512, 512), 512)
    load_q = local(queries.at[:, q_cols], q_buf.at[core], 5)
    load_t = []
    for number, table in enumerate((cosine, sine)):
        load_t.append(local(table, tables.at[number], 6 + number))

    peers = [at(y + dy, xl if dx == 0 else 1 - xl, core) for dy, dx in PLANE]
    peers += [near["core"], near["mate2"], near["xh"], near["z+"], near["z-"]]
    barrier = pltpu.get_barrier_semaphore()
    for peer in peers:
        pl.semaphore_signal(barrier, inc=1, device_id=peer, device_id_type=MESH)
    pl.semaphore_wait(barrier, len(peers))

    sends = []

    def send(src, dst, number, device):
        copy = remote(src, dst, number, device)
        copy.start()
        sends.append(copy)

    for copy in load_w:
        copy.wait()
    other = (z * 2 + 1 - xh) * 2

    def piece(zz, flip, half):
        aa = 1 - xh if flip else xh
        return (zz % 8 * 2 + aa) * 2 + half

    def part(distance, ring):
        if distance < 4:
            return pl.ds(0, 128)
        return pl.ds(ring * 64, 64)

    def ring_send(ring, distance, flip):
        source = z - (distance - 1) if ring == 0 else z + (distance - 1)
        ref = w_buf.at[piece(source + 8, flip, side), part(distance, ring), :]
        send(ref, ref, EV_Z + event(ring, distance, flip), near["z+" if ring == 0 else "z-"])

    send(w_buf.at[own + 1 - side], w_buf.at[own + 1 - side], EV_XH, near["xh"])
    for ring in range(2):
        ring_send(ring, 1, 0)
    send(w_buf.at[own + side], w_buf.at[own + side], EV_XH + 1, near["xh"])
    send(states, x_buf.at[my_rows, :], EV_X, near["core"])

    landing = w_buf.at[other + side]
    remote(landing, landing, EV_XH, near["xh"]).wait_recv()
    for ring in range(2):
        ring_send(ring, 1, 1)

    flags = jnp.broadcast_to(marks[...].astype(F32), (128, 256))
    m_buf[core] = jnp.transpose(flags).astype(BF16)

    def q_at(kv_head):
        return queries.at[:, pl.ds(pl.multiple_of(kv_head * 512, 512), 512)]

    send(q_at(2 * (1 - core) + role), q_buf.at[core], EV_Q, near["core"])
    send(m_buf.at[core], m_buf.at[core], EV_M, near["core"])
    send(m_buf.at[core], m_buf.at[2 + core], EV_M + 1, near["mate"])
    send(m_buf.at[core], m_buf.at[2 + core], EV_M + 2, near["mate2"])

    def project(zz, first=False):
        zz = zz % 8
        weights = w_buf[pl.ds(zz * 4, 4)].reshape(512, 512)
        rows = x_buf[:, pl.ds(pl.multiple_of(zz * 512, 512), 512)]
        term = jnp.dot(rows, weights, preferred_element_type=F32)
        if first:
            sums[...] = term
        else:
            sums[...] += term

    def plane_wait(distance):
        for ring in range(2):
            source = z - distance if ring == 0 else z + distance
            for flip in range(2):
                way = ROUTE[ring, distance, flip]
                ref = w_buf.at[piece(source + 8, flip, 1 - side), part(distance, ring), :]
                remote(ref, ref, EV_P + event(ring, distance, flip), near[way]).wait_recv()

    for distance in range(1, 5):
        for flip in range(2):
            for ring in range(2):
                source = z - distance if ring == 0 else z + distance
                ref = w_buf.at[piece(source + 8, flip, side), part(distance, ring), :]
                number = event(ring, distance, flip)
                remote(ref, ref, EV_Z + number, near["z-" if ring == 0 else "z+"]).wait_recv()
                if distance < 4:
                    ring_send(ring, distance + 1, flip)
                way = ROUTE[ring, distance, flip]
                if way != "xh":
                    send(ref, ref, EV_P + number, near[way])
                elif flip == 1:
                    for mine in range(2):
                        ref = w_buf.at[piece(source + 8, 1 - mine, side), part(distance, ring), :]
                        send(ref, ref, EV_P + event(ring, distance, mine), near["xh"])
        if distance == 1:
            mask_rows = mask_row[...].astype(F32)
            for i in range(32):
                wide_row = jnp.broadcast_to(mask_rows[i : i + 1, :], (16, 128))
                x_buf[pl.ds(512, 16), pl.ds(i * 128, 128)] = wide_row.astype(BF16)

            for copy in load_t:
                copy.wait()
            near_c, near_s = tables[0], tables[1]
            for pair, where in ((1, mate), (0, chip)):
                far_c, far_s = far_cosine[pl.ds(where, 1), :], far_sine[pl.ds(where, 1), :]
                tables[pair * 2] = near_c * far_c - near_s * far_s
                tables[pair * 2 + 1] = near_s * far_c + near_c * far_s
            load_x.wait()
            theirs = x_buf.at[pl.ds(pl.multiple_of((1 - core) * 256, 256), 256), :]
            remote(theirs, theirs, EV_X, near["core"]).wait_recv()
            landing = w_buf.at[other + 1 - side]
            remote(landing, landing, EV_XH + 1, near["xh"]).wait_recv()
            project(z, True)
            send(q_at(2 * core + 1 - role), q_buf.at[2 + core], EV_Q + 1, near["mate"])
            send(q_at(2 * (1 - core) + 1 - role), q_buf.at[2 + core], EV_Q + 2, near["mate2"])
        else:
            plane_wait(distance - 1)
            project(z + 8 - distance + 1)
            project(z + distance - 1)
            if distance == 3:
                v_all[:, pl.ds(128, 128)] = jnp.ones((v_all.shape[0], 128), BF16)
                row_max[...] = jnp.full(row_max.shape, -1e30, F32)
                mix[...] = jnp.zeros(mix.shape, F32)
    plane_wait(4)
    project(z + 4)

    def rotate(rows, pair, first, count):
        turned = pltpu.roll(rows, 64, 1)
        span = pl.ds(first, count)
        return rows * tables[pair * 2, span, :] + turned * tables[pair * 2 + 1, span, :]

    for kind in range(2):
        keys = sums[pl.ds(0, 512), pl.ds(kind * 128, 128)]
        k_own[kind] = rotate(keys, 0, 0, 512).astype(BF16)
        v_own[kind] = sums[pl.ds(0, 512), pl.ds(256 + kind * 128, 128)].astype(BF16)

    def kv_rows(where):
        return pl.ds(pl.multiple_of(where * 512, 512), 512)

    def k_at(where):
        return k_all.at[kv_rows(where), :]

    def v_at(where):
        return v_all.at[kv_rows(where), pl.ds(0, 128)]

    beside = y * 2 + 1 - xl

    def seen(dy, source_y):
        return jnp.logical_not((source_y == 3) & ((dy == 2) | (dy == 3)))

    def hop(dy):
        return at(y + dy, xl, core)

    send(v_own.at[1 - role], v_relay, EV_V, near["xl"])
    send(k_own.at[role], k_at(chip), EV_K + 1, near["xl"])
    send(v_own.at[role], v_at(chip), EV_V + 1, near["xl"])

    def first_hop(dy, values):
        kind = (role + dy) % 2
        if values:
            return remote(v_own.at[kind], v_at(chip), EV_V + dy * 2, hop(dy))
        return remote(k_own.at[kind], k_at(chip), EV_K + dy * 2, hop(dy))

    def second_hop_v(dy):
        source = v_at(beside) if dy == 2 else v_relay
        return remote(source, v_at(beside), EV_V + dy * 2 + 1, hop(dy))

    def second_hop_k(dy):
        rows = k_at((y + 4 - dy) % 4 * 2 + xl)
        return remote(rows, rows, EV_K + dy * 2 + 1, near["xl"])

    for dy, values in ((1, 0), (3, 0), (1, 1), (3, 1), (2, 0), (2, 1)):
        @pl.when(seen(dy, y))
        def _():
            first_hop(dy, values).start()

    k_all[kv_rows(chip), :] = k_own[role]
    v_all[kv_rows(chip), pl.ds(0, 128)] = v_own[role]

    load_q.wait()
    for number, slot, device in (
        (EV_Q, 1 - core, near["core"]),
        (EV_Q + 1, 2 + core, near["mate"]),
        (EV_Q + 2, 3 - core, near["mate2"]),
    ):
        remote(q_buf.at[slot], q_buf.at[slot], number, device).wait_recv()
        mark = number - EV_Q + EV_M
        remote(m_buf.at[slot], m_buf.at[slot], mark, device).wait_recv()

    mask_key = sums[pl.ds(512, 16), pl.ds(pl.multiple_of(role * 128, 128), 128)]
    mask_value = sums[pl.ds(512, 16), pl.ds(pl.multiple_of(256 + role * 128, 128), 128)]
    mask_key = jnp.broadcast_to(mask_key[0:1, :], (256, 128))
    mask_value = jnp.broadcast_to(mask_value[0:1, :], (256, 128)).astype(BF16).astype(F32)

    def build(pair):
        where = mate if pair else chip
        for i in range(2):
            slot = pair * 2 + i
            base = 4096 + slot * 512
            block = pl.ds(pl.multiple_of(where * 512 + i * 256, 256), 256)
            masked = m_buf[slot].astype(F32) > 0.5
            noisy_k = jnp.where(
                masked, rotate(mask_key, pair, i * 256, 256), k_all[block, :].astype(F32)
            ).astype(BF16)
            noisy_v = jnp.where(
                masked, mask_value, v_all[block, pl.ds(0, 128)].astype(F32)
            ).astype(BF16)
            noisy = pl.ds(base + i * 256, 256)
            k_all[noisy, :] = noisy_k
            v_all[noisy, pl.ds(0, 128)] = noisy_v
            if i == 0:
                k_all[pl.ds(base + 256, 256), :] = noisy_k
                v_all[pl.ds(base + 256, 256), :] = jnp.zeros((256, 256), BF16)
            else:
                before = pl.ds(pl.multiple_of(where * 512, 512), 256)
                k_all[pl.ds(base, 256), :] = k_all[before, :]
                v_all[pl.ds(base, 256), pl.ds(0, 128)] = v_all[before, pl.ds(0, 128)]

    def absorb(slot, start):
        span = pl.ds(pl.multiple_of(start, 512), 512)
        for tile in range(8):
            query = q_buf[slot, pl.ds(tile % 2 * 128, 128), pl.ds(tile // 2 * 128, 128)]
            scores = lax.dot_general(query, k_all[span, :], NT, preferred_element_type=F32)
            before = row_max[slot * 8 + tile]
            after = jnp.maximum(before, jnp.max(scores, 1, keepdims=True))
            shrink = jnp.exp2((before - after) * SCORE_SCALE)
            probs = jnp.exp2((scores - jnp.tile(after, (1, 4))) * SCORE_SCALE).astype(BF16)
            term = jnp.dot(probs, v_all[span, :], preferred_element_type=F32)
            total = mix[slot * 8 + tile]
            mix[slot * 8 + tile] = total * jnp.tile(shrink, (1, 2)) + term
            row_max[slot * 8 + tile] = after

    def finish(slot):
        for tile in range(8):
            total = mix[slot * 8 + tile]
            o_buf[slot, pl.ds(tile % 2 * 128, 128), pl.ds(tile // 2 * 128, 128)] = (
                total[:, :128] / total[:, 128:]
            ).astype(BF16)

    out_cols = pl.ds(pl.multiple_of(head * 512, 512), 512)

    def mate_out(i):
        number = EV_O + (i - core + 2) % 2
        return remote(o_buf.at[2 + i], out.at[:, out_cols], number, at(3 - y, xl, i))

    late = (y == 0) | (y == 2)

    def source_of(turn):
        dy = jnp.where(turn >= 6, 2, jnp.where((turn == 0) | (turn == 3), 0, jnp.where((turn == 1) | (turn == 4), 1, 3)))
        dx = jnp.where((turn == 3) | (turn == 4) | (turn == 5) | (turn == 7), 1, 0)
        source_y = (y + 4 - dy) % 4
        return dy, dx, source_y, source_y * 2 + jnp.where(dx == 0, xl, 1 - xl)

    def visit(number, carry):
        turn = number % 8
        first = number < 8
        dy, dx, source_y, source = source_of(turn)
        here = first & seen(dy, source_y)
        device = near["xl"]

        def pass_on_k(hop_y):
            @pl.when(seen(hop_y, (y + 4 - hop_y) % 4))
            def _():
                rows = k_at((y + 4 - hop_y) % 4 * 2 + xl)
                remote(rows, rows, EV_K + hop_y * 2, device).wait_recv()
                second_hop_k(hop_y).start()

        def pass_on_v(hop_y):
            @pl.when(seen(hop_y, y))
            def _():
                second_hop_v(hop_y).start()

        @pl.when(number == 1)
        def _():
            remote(v_relay, v_relay, EV_V, device).wait_recv()
            pass_on_v(1)
            pass_on_v(3)
            pass_on_k(1)
            pass_on_k(3)

        @pl.when(number == 3)
        def _():
            remote(v_at(beside), v_at(beside), EV_V + 1, device).wait_recv()
            pass_on_v(2)
            pass_on_k(2)

        @pl.when(here & (dx == 1))
        def _():
            remote(k_at(source), k_at(source), EV_K + dy * 2 + 1, device).wait_recv()

        @pl.when(here & (turn != 0) & (turn != 3))
        def _():
            remote(v_at(source), v_at(source), EV_V + dy * 2 + dx, device).wait_recv()

        @pl.when(number == 0)
        def _():
            build(0)

        @pl.when(first & (source == mate))
        def _():
            build(1)

        def item(index, carry):
            both = turn == 7
            slot = (jnp.where(both, index // 2, index) + 2) % 4
            _, _, _, earlier = source_of(6)
            origin = jnp.where(both & (index % 2 == 0), earlier, source)
            other_pair = slot >= 2
            level = jnp.where(other_pair, mate, chip)
            turn_now = jnp.where(other_pair | (y >= 2), first, jnp.logical_not(first))

            @pl.when(turn_now & (origin <= level))
            def _():
                absorb(slot, jnp.where(origin == level, 4096 + slot * 512, origin * 512))

            done = number == jnp.where(late, 7, 5)

            @pl.when(other_pair & done & ((turn < 7) | (index % 2 == 1)))
            def _():
                finish(slot)
                mate_out(slot - 2).start()

            return carry

        lax.fori_loop(0, jnp.where(turn < 6, 4, jnp.where(turn == 6, 0, 8)), item, 0)
        return carry

    lax.fori_loop(0, jnp.where(y < 2, 16, 8), visit, 0)
    for i in range(2):
        finish(i)
    send(o_buf.at[1 - core], out.at[:, out_cols], EV_O + 2, near["core"])
    store = local(o_buf.at[core], out.at[:, out_cols], 5)
    store.wait()

    def o_at(kv_head):
        return out.at[:, pl.ds(pl.multiple_of(kv_head * 512, 512), 512)]

    for number, kv_head, device in (
        (EV_O, 2 * core + 1 - role, near["mate"]),
        (EV_O + 1, 2 * (1 - core) + 1 - role, near["mate2"]),
        (EV_O + 2, 2 * (1 - core) + role, near["core"]),
    ):
        remote(o_at(kv_head), o_at(kv_head), number, device).wait_recv()
    for i in range(2):
        mate_out(i).wait_send()
    for dy in (1, 2, 3):
        @pl.when(seen(dy, y))
        def _():
            for values in range(2):
                first_hop(dy, values).wait_send()
            second_hop_v(dy).wait_send()

        @pl.when(seen(dy, (y + 4 - dy) % 4))
        def _():
            second_hop_k(dy).wait_send()
    for copy in sends:
        copy.wait_send()


def tables_of(positions):
    half = HEAD_DIM // 2
    steps = np.arange(half, dtype=np.float32) * np.float32(2.0) / np.float32(HEAD_DIM)
    frequency = (np.float32(ROPE_BASE) ** (-steps)).astype(np.float64)
    angles = positions.astype(np.float64)[:, None] * frequency[None, :]
    cosine = np.cos(angles).astype(np.float32)
    sine = np.sin(angles).astype(np.float32)
    return jnp.asarray(np.concatenate([cosine, cosine], 1)), jnp.asarray(np.concatenate([-sine, sine], 1))


def solution(mesh):
    def shards(clean_states, noise_mask, mask_embed, queries, w_key, w_value):
        _, rows, width = clean_states.shape
        cosine, sine = tables_of(np.arange(2 * rows))
        far_cosine, far_sine = tables_of(np.arange(8) * 2 * rows)
        any_ = pl.BlockSpec(memory_space=pl.ANY)
        vmem = pl.BlockSpec(memory_space=pltpu.VMEM)
        output = pl.pallas_call(
            kernel,
            out_shape=pltpu.VMEM((256, 2048), BF16),
            in_specs=[any_, vmem, vmem, any_, any_, any_, any_, any_, vmem, vmem],
            out_specs=vmem,
            scratch_shapes=[
                pltpu.VMEM((528, 4096), BF16),
                pltpu.VMEM((32, 128, 512), BF16),
                pltpu.VMEM((528, 512), F32),
                pltpu.VMEM((2, 512, 128), BF16),
                pltpu.VMEM((2, 512, 128), BF16),
                pltpu.VMEM((512, 128), BF16),
                pltpu.VMEM((6144, 128), BF16),
                pltpu.VMEM((6144, 256), BF16),
                pltpu.VMEM((4, 256, 512), BF16),
                pltpu.VMEM((4, 256, 128), BF16),
                pltpu.VMEM((4, 256, 512), BF16),
                pltpu.VMEM((4, 512, 128), F32),
                pltpu.VMEM((32, 128, 128), F32),
                pltpu.VMEM((32, 128, 256), F32),
                pltpu.SemaphoreType.DMA((EV_COUNT,)),
                pltpu.SemaphoreType.DMA((EV_COUNT,)),
                pltpu.SemaphoreType.DMA((10,)),
            ],
            compiler_params=pltpu.CompilerParams(
                collective_id=0, has_side_effects=True, vmem_limit_bytes=56 << 20
            ),
        )(
            clean_states[0], noise_mask, mask_embed.reshape(32, 128), queries[0],
            w_key, w_value, cosine, sine, far_cosine, far_sine,
        )
        return output[None]

    placed = (
        P("fsdp", "seq", None),
        P("fsdp", "seq"),
        P(),
        P("fsdp", "seq", None),
        P("fsdp", None),
        P("fsdp", None),
    )
    return jax.shard_map(
        shards, mesh=mesh, in_specs=placed, out_specs=P("fsdp", "seq", None), check_vma=False
    )
```

```python
import jax
import jax.numpy as jnp
import numpy as np
from jax import lax
from jax.experimental import pallas as pl
from jax.experimental.pallas import tpu as pltpu
from jax.sharding import PartitionSpec as P

MESH = pl.DeviceIdType.MESH
BF16 = jnp.bfloat16
F32 = jnp.float32
HEAD_DIM = 128
BLOCK = 256
ROPE_BASE = 500000.0
SCORE_SCALE = float(HEAD_DIM**-0.5 * np.log2(np.e))
NT = (((1,), (1,)), ((), ()))

ROUTE = {
    (0, 1, 0): "buddy", (0, 1, 1): "xl", (1, 1, 0): "buddy", (1, 1, 1): "xl",
    (0, 2, 0): "buddy", (0, 2, 1): "xl", (1, 2, 0): "xh", (1, 2, 1): "xh",
    (0, 3, 0): "buddy", (0, 3, 1): "xl", (1, 3, 0): "mate", (1, 3, 1): "xl",
    (0, 4, 0): "buddy", (0, 4, 1): "xl", (1, 4, 0): "mate", (1, 4, 1): "buddy",
}
PLANE = ((0, 1), (1, 0), (3, 0), (1, 1), (3, 1), (2, 0), (2, 1))

EV_X, EV_XH, EV_Z, EV_P = 0, 1, 3, 19
EV_Q, EV_M, EV_K, EV_V, EV_O = 35, 38, 41, 49, 57
EV_COUNT = 60


def event(ring, distance, other):
    return (ring * 4 + distance - 1) * 2 + other


def kernel(
    states, marks, mask_row, queries, w_key, w_value, cosine, sine, far_cosine, far_sine, out,
    x_buf, w_buf, sums, k_own, v_own, v_relay, k_all, v_all, q_buf, m_buf, o_buf,
    tables, row_max, mix, send_sem, recv_sem, local_sem,
):
    seq = lax.axis_index("seq")
    fsdp = lax.axis_index("fsdp")
    core = seq % 2
    chip = seq // 2
    xl = chip % 2
    y = chip // 2
    z = fsdp // 2
    xh = fsdp % 2
    role = y % 2
    side = (y + xl) % 2
    mate = (3 - y) * 2 + xl

    def at(yy, xx, cc):
        return ((yy % 4 * 2 + xx) * 2 + cc, fsdp)

    near = {
        "buddy": at(y // 2 * 2 + 1 - y % 2, xl, core),
        "xl": at(y, 1 - xl, core),
        "xh": (at(y, 1 - xl, core)[0], z * 2 + 1 - xh),
        "z+": (seq, (z + 1) % 8 * 2 + xh),
        "z-": (seq, (z + 7) % 8 * 2 + xh),
        "core": at(y, xl, 1 - core),
        "mate": at(3 - y, xl, core),
        "mate2": at(3 - y, xl, 1 - core),
    }

    def remote(src, dst, number, device):
        return pltpu.make_async_remote_copy(
            src, dst, send_sem.at[number], recv_sem.at[number],
            device_id=device, device_id_type=MESH,
        )

    locals_ = []

    def local(src, dst, number):
        copy = pltpu.make_async_copy(src, dst, local_sem.at[number])
        copy.start()
        return copy

    wide = pl.ds(pl.multiple_of(core * 256, 256), 256)
    own = fsdp * 2
    load_w = []
    for half in range(2):
        rows = pl.ds(half * 128, 128)
        load_w.append(local(w_key.at[rows, wide], w_buf.at[own + half, :, pl.ds(0, 256)], half * 2))
        load_w.append(local(w_value.at[rows, wide], w_buf.at[own + half, :, pl.ds(256, 256)], half * 2 + 1))
    my_rows = pl.ds(pl.multiple_of(core * 256, 256), 256)
    load_x = local(states, x_buf.at[my_rows, :], 4)
    head = 2 * core + role
    q_cols = pl.ds(pl.multiple_of(head * 512, 512), 512)
    load_q = local(queries.at[:, q_cols], q_buf.at[core], 5)
    load_t = []
    for number, table in enumerate((cosine, sine)):
        load_t.append(local(table, tables.at[number], 6 + number))

    peers = [at(y + dy, xl if dx == 0 else 1 - xl, core) for dy, dx in PLANE]
    peers += [near["core"], near["mate2"], near["xh"], near["z+"], near["z-"]]
    barrier = pltpu.get_barrier_semaphore()
    for peer in peers:
        pl.semaphore_signal(barrier, inc=1, device_id=peer, device_id_type=MESH)
    pl.semaphore_wait(barrier, len(peers))

    sends = []

    def send(src, dst, number, device):
        copy = remote(src, dst, number, device)
        copy.start()
        sends.append(copy)

    for copy in load_w:
        copy.wait()
    other = (z * 2 + 1 - xh) * 2

    def piece(zz, flip, half):
        aa = 1 - xh if flip else xh
        return (zz % 8 * 2 + aa) * 2 + half

    def part(distance, ring):
        if distance < 4:
            return pl.ds(0, 128)
        return pl.ds(ring * 64, 64)

    def ring_send(ring, distance, flip):
        source = z - (distance - 1) if ring == 0 else z + (distance - 1)
        ref = w_buf.at[piece(source + 8, flip, side), part(distance, ring), :]
        send(ref, ref, EV_Z + event(ring, distance, flip), near["z+" if ring == 0 else "z-"])

    send(w_buf.at[own + 1 - side], w_buf.at[own + 1 - side], EV_XH, near["xh"])
    for ring in range(2):
        ring_send(ring, 1, 0)
    send(w_buf.at[own + side], w_buf.at[own + side], EV_XH + 1, near["xh"])
    send(states, x_buf.at[my_rows, :], EV_X, near["core"])

    landing = w_buf.at[other + side]
    remote(landing, landing, EV_XH, near["xh"]).wait_recv()
    for ring in range(2):
        ring_send(ring, 1, 1)

    flags = jnp.broadcast_to(marks[...].astype(F32), (128, 256))
    m_buf[core] = jnp.transpose(flags).astype(BF16)

    def q_at(kv_head):
        return queries.at[:, pl.ds(pl.multiple_of(kv_head * 512, 512), 512)]

    send(q_at(2 * (1 - core) + role), q_buf.at[core], EV_Q, near["core"])
    send(m_buf.at[core], m_buf.at[core], EV_M, near["core"])
    send(m_buf.at[core], m_buf.at[2 + core], EV_M + 1, near["mate"])
    send(m_buf.at[core], m_buf.at[2 + core], EV_M + 2, near["mate2"])

    def project(zz, first=False):
        zz = zz % 8
        weights = w_buf[pl.ds(zz * 4, 4)].reshape(512, 512)
        rows = x_buf[:, pl.ds(pl.multiple_of(zz * 512, 512), 512)]
        term = jnp.dot(rows, weights, preferred_element_type=F32)
        if first:
            sums[...] = term
        else:
            sums[...] += term

    def plane_wait(distance):
        for ring in range(2):
            source = z - distance if ring == 0 else z + distance
            for flip in range(2):
                way = ROUTE[ring, distance, flip]
                ref = w_buf.at[piece(source + 8, flip, 1 - side), part(distance, ring), :]
                remote(ref, ref, EV_P + event(ring, distance, flip), near[way]).wait_recv()

    for distance in range(1, 5):
        for flip in range(2):
            for ring in range(2):
                source = z - distance if ring == 0 else z + distance
                ref = w_buf.at[piece(source + 8, flip, side), part(distance, ring), :]
                number = event(ring, distance, flip)
                remote(ref, ref, EV_Z + number, near["z-" if ring == 0 else "z+"]).wait_recv()
                if distance < 4:
                    ring_send(ring, distance + 1, flip)
                way = ROUTE[ring, distance, flip]
                if way != "xh":
                    send(ref, ref, EV_P + number, near[way])
                elif flip == 1:
                    for mine in range(2):
                        ref = w_buf.at[piece(source + 8, 1 - mine, side), part(distance, ring), :]
                        send(ref, ref, EV_P + event(ring, distance, mine), near["xh"])
        if distance == 1:
            mask_rows = mask_row[...].astype(F32)
            for i in range(32):
                wide_row = jnp.broadcast_to(mask_rows[i : i + 1, :], (16, 128))
                x_buf[pl.ds(512, 16), pl.ds(i * 128, 128)] = wide_row.astype(BF16)

            for copy in load_t:
                copy.wait()
            near_c, near_s = tables[0], tables[1]
            for pair, where in ((1, mate), (0, chip)):
                far_c, far_s = far_cosine[pl.ds(where, 1), :], far_sine[pl.ds(where, 1), :]
                tables[pair * 2] = near_c * far_c - near_s * far_s
                tables[pair * 2 + 1] = near_s * far_c + near_c * far_s
            load_x.wait()
            theirs = x_buf.at[pl.ds(pl.multiple_of((1 - core) * 256, 256), 256), :]
            remote(theirs, theirs, EV_X, near["core"]).wait_recv()
            landing = w_buf.at[other + 1 - side]
            remote(landing, landing, EV_XH + 1, near["xh"]).wait_recv()
            project(z, True)
            send(q_at(2 * core + 1 - role), q_buf.at[2 + core], EV_Q + 1, near["mate"])
            send(q_at(2 * (1 - core) + 1 - role), q_buf.at[2 + core], EV_Q + 2, near["mate2"])
        else:
            plane_wait(distance - 1)
            project(z + 8 - distance + 1)
            project(z + distance - 1)
            if distance == 3:
                v_all[:, pl.ds(128, 128)] = jnp.ones((v_all.shape[0], 128), BF16)
                row_max[...] = jnp.full(row_max.shape, -1e30, F32)
                mix[...] = jnp.zeros(mix.shape, F32)
    plane_wait(4)
    project(z + 4)

    def rotate(rows, pair, first, count):
        turned = pltpu.roll(rows, 64, 1)
        span = pl.ds(first, count)
        return rows * tables[pair * 2, span, :] + turned * tables[pair * 2 + 1, span, :]

    def kv_rows(where):
        return pl.ds(pl.multiple_of(where * 512, 512), 512)

    def k_at(where):
        return k_all.at[kv_rows(where), :]

    def v_at(where):
        return v_all.at[kv_rows(where), pl.ds(0, 128)]

    beside = y * 2 + 1 - xl

    def seen(dy, source_y):
        return jnp.logical_not((source_y == 3) & ((dy == 2) | (dy == 3)))

    def hop(dy):
        return at(y + dy, xl, core)

    for kind in range(2):
        v_own[kind] = sums[pl.ds(0, 512), pl.ds(256 + kind * 128, 128)].astype(BF16)
    send(v_own.at[1 - role], v_relay, EV_V, near["xl"])
    for kind in range(2):
        keys = sums[pl.ds(0, 512), pl.ds(kind * 128, 128)]
        k_own[kind] = rotate(keys, 0, 0, 512).astype(BF16)
    send(k_own.at[role], k_at(chip), EV_K + 1, near["xl"])
    send(v_own.at[role], v_at(chip), EV_V + 1, near["xl"])

    def first_hop(dy, values):
        kind = (role + dy) % 2
        if values:
            return remote(v_own.at[kind], v_at(chip), EV_V + dy * 2, hop(dy))
        return remote(k_own.at[kind], k_at(chip), EV_K + dy * 2, hop(dy))

    def second_hop_v(dy):
        source = v_at(beside) if dy == 2 else v_relay
        return remote(source, v_at(beside), EV_V + dy * 2 + 1, hop(dy))

    def second_hop_k(dy):
        rows = k_at((y + 4 - dy) % 4 * 2 + xl)
        return remote(rows, rows, EV_K + dy * 2 + 1, near["xl"])

    for dy, values in ((1, 0), (3, 0), (1, 1), (3, 1), (2, 0), (2, 1)):
        @pl.when(seen(dy, y))
        def _():
            first_hop(dy, values).start()

    k_all[kv_rows(chip), :] = k_own[role]
    v_all[kv_rows(chip), pl.ds(0, 128)] = v_own[role]

    load_q.wait()
    for number, slot, device in (
        (EV_Q, 1 - core, near["core"]),
        (EV_Q + 1, 2 + core, near["mate"]),
        (EV_Q + 2, 3 - core, near["mate2"]),
    ):
        remote(q_buf.at[slot], q_buf.at[slot], number, device).wait_recv()
        mark = number - EV_Q + EV_M
        remote(m_buf.at[slot], m_buf.at[slot], mark, device).wait_recv()

    mask_key = sums[pl.ds(512, 16), pl.ds(pl.multiple_of(role * 128, 128), 128)]
    mask_value = sums[pl.ds(512, 16), pl.ds(pl.multiple_of(256 + role * 128, 128), 128)]
    mask_key = jnp.broadcast_to(mask_key[0:1, :], (256, 128))
    mask_value = jnp.broadcast_to(mask_value[0:1, :], (256, 128)).astype(BF16).astype(F32)

    def build(pair):
        where = mate if pair else chip
        for i in range(2):
            slot = pair * 2 + i
            base = 4096 + slot * 512
            block = pl.ds(pl.multiple_of(where * 512 + i * 256, 256), 256)
            masked = m_buf[slot].astype(F32) > 0.5
            noisy_k = jnp.where(
                masked, rotate(mask_key, pair, i * 256, 256), k_all[block, :].astype(F32)
            ).astype(BF16)
            noisy_v = jnp.where(
                masked, mask_value, v_all[block, pl.ds(0, 128)].astype(F32)
            ).astype(BF16)
            noisy = pl.ds(base + i * 256, 256)
            k_all[noisy, :] = noisy_k
            v_all[noisy, pl.ds(0, 128)] = noisy_v
            if i == 0:
                k_all[pl.ds(base + 256, 256), :] = noisy_k
                v_all[pl.ds(base + 256, 256), :] = jnp.zeros((256, 256), BF16)
            else:
                before = pl.ds(pl.multiple_of(where * 512, 512), 256)
                k_all[pl.ds(base, 256), :] = k_all[before, :]
                v_all[pl.ds(base, 256), pl.ds(0, 128)] = v_all[before, pl.ds(0, 128)]

    def absorb(slot, start):
        span = pl.ds(pl.multiple_of(start, 512), 512)
        for tile in range(8):
            query = q_buf[slot, pl.ds(tile % 2 * 128, 128), pl.ds(tile // 2 * 128, 128)]
            scores = lax.dot_general(query, k_all[span, :], NT, preferred_element_type=F32)
            before = row_max[slot * 8 + tile]
            after = jnp.maximum(before, jnp.max(scores, 1, keepdims=True))
            shrink = jnp.exp2((before - after) * SCORE_SCALE)
            probs = jnp.exp2((scores - jnp.tile(after, (1, 4))) * SCORE_SCALE).astype(BF16)
            term = jnp.dot(probs, v_all[span, :], preferred_element_type=F32)
            total = mix[slot * 8 + tile]
            mix[slot * 8 + tile] = total * jnp.tile(shrink, (1, 2)) + term
            row_max[slot * 8 + tile] = after

    def finish(slot):
        for tile in range(8):
            total = mix[slot * 8 + tile]
            o_buf[slot, pl.ds(tile % 2 * 128, 128), pl.ds(tile // 2 * 128, 128)] = (
                total[:, :128] / total[:, 128:]
            ).astype(BF16)

    out_cols = pl.ds(pl.multiple_of(head * 512, 512), 512)

    def mate_out(i):
        number = EV_O + (i - core + 2) % 2
        return remote(o_buf.at[2 + i], out.at[:, out_cols], number, at(3 - y, xl, i))

    late = (y == 0) | (y == 2)

    def source_of(turn):
        dy = jnp.where(turn >= 6, 2, jnp.where((turn == 0) | (turn == 3), 0, jnp.where((turn == 1) | (turn == 4), 1, 3)))
        dx = jnp.where((turn == 3) | (turn == 4) | (turn == 5) | (turn == 7), 1, 0)
        source_y = (y + 4 - dy) % 4
        return dy, dx, source_y, source_y * 2 + jnp.where(dx == 0, xl, 1 - xl)

    def visit(number, carry):
        turn = number % 8
        first = number < 8
        dy, dx, source_y, source = source_of(turn)
        here = first & seen(dy, source_y)
        device = near["xl"]

        def pass_on_k(hop_y):
            @pl.when(seen(hop_y, (y + 4 - hop_y) % 4))
            def _():
                rows = k_at((y + 4 - hop_y) % 4 * 2 + xl)
                remote(rows, rows, EV_K + hop_y * 2, device).wait_recv()
                second_hop_k(hop_y).start()

        def pass_on_v(hop_y):
            @pl.when(seen(hop_y, y))
            def _():
                second_hop_v(hop_y).start()

        @pl.when(number == 1)
        def _():
            remote(v_relay, v_relay, EV_V, device).wait_recv()
            pass_on_v(1)
            pass_on_v(3)
            pass_on_k(1)
            pass_on_k(3)

        @pl.when(number == 3)
        def _():
            remote(v_at(beside), v_at(beside), EV_V + 1, device).wait_recv()
            pass_on_v(2)
            pass_on_k(2)

        @pl.when(here & (dx == 1))
        def _():
            remote(k_at(source), k_at(source), EV_K + dy * 2 + 1, device).wait_recv()

        @pl.when(here & (turn != 0) & (turn != 3))
        def _():
            remote(v_at(source), v_at(source), EV_V + dy * 2 + dx, device).wait_recv()

        @pl.when(number == 0)
        def _():
            build(0)

        @pl.when(first & (source == mate))
        def _():
            build(1)

        def item(index, carry):
            both = turn == 7
            slot = (jnp.where(both, index // 2, index) + 2) % 4
            _, _, _, earlier = source_of(6)
            origin = jnp.where(both & (index % 2 == 0), earlier, source)
            other_pair = slot >= 2
            level = jnp.where(other_pair, mate, chip)
            turn_now = jnp.where(other_pair | (y >= 2), first, jnp.logical_not(first))

            @pl.when(turn_now & (origin <= level))
            def _():
                absorb(slot, jnp.where(origin == level, 4096 + slot * 512, origin * 512))

            done = number == jnp.where(late, 7, 5)

            @pl.when(other_pair & done & ((turn < 7) | (index % 2 == 1)))
            def _():
                finish(slot)
                mate_out(slot - 2).start()

            return carry

        lax.fori_loop(0, jnp.where(turn < 6, 4, jnp.where(turn == 6, 0, 8)), item, 0)
        return carry

    lax.fori_loop(0, jnp.where(y < 2, 16, 8), visit, 0)
    for i in range(2):
        finish(i)
    send(o_buf.at[1 - core], out.at[:, out_cols], EV_O + 2, near["core"])
    store = local(o_buf.at[core], out.at[:, out_cols], 5)
    store.wait()

    def o_at(kv_head):
        return out.at[:, pl.ds(pl.multiple_of(kv_head * 512, 512), 512)]

    for number, kv_head, device in (
        (EV_O, 2 * core + 1 - role, near["mate"]),
        (EV_O + 1, 2 * (1 - core) + 1 - role, near["mate2"]),
        (EV_O + 2, 2 * (1 - core) + role, near["core"]),
    ):
        remote(o_at(kv_head), o_at(kv_head), number, device).wait_recv()
    for i in range(2):
        mate_out(i).wait_send()
    for dy in (1, 2, 3):
        @pl.when(seen(dy, y))
        def _():
            for values in range(2):
                first_hop(dy, values).wait_send()
            second_hop_v(dy).wait_send()

        @pl.when(seen(dy, (y + 4 - dy) % 4))
        def _():
            second_hop_k(dy).wait_send()
    for copy in sends:
        copy.wait_send()


def tables_of(positions):
    half = HEAD_DIM // 2
    steps = np.arange(half, dtype=np.float32) * np.float32(2.0) / np.float32(HEAD_DIM)
    frequency = (np.float32(ROPE_BASE) ** (-steps)).astype(np.float64)
    angles = positions.astype(np.float64)[:, None] * frequency[None, :]
    cosine = np.cos(angles).astype(np.float32)
    sine = np.sin(angles).astype(np.float32)
    return jnp.asarray(np.concatenate([cosine, cosine], 1)), jnp.asarray(np.concatenate([-sine, sine], 1))


def solution(mesh):
    def shards(clean_states, noise_mask, mask_embed, queries, w_key, w_value):
        _, rows, width = clean_states.shape
        cosine, sine = tables_of(np.arange(2 * rows))
        far_cosine, far_sine = tables_of(np.arange(8) * 2 * rows)
        any_ = pl.BlockSpec(memory_space=pl.ANY)
        vmem = pl.BlockSpec(memory_space=pltpu.VMEM)
        output = pl.pallas_call(
            kernel,
            out_shape=pltpu.VMEM((256, 2048), BF16),
            in_specs=[any_, vmem, vmem, any_, any_, any_, any_, any_, vmem, vmem],
            out_specs=vmem,
            scratch_shapes=[
                pltpu.VMEM((528, 4096), BF16),
                pltpu.VMEM((32, 128, 512), BF16),
                pltpu.VMEM((528, 512), F32),
                pltpu.VMEM((2, 512, 128), BF16),
                pltpu.VMEM((2, 512, 128), BF16),
                pltpu.VMEM((512, 128), BF16),
                pltpu.VMEM((6144, 128), BF16),
                pltpu.VMEM((6144, 256), BF16),
                pltpu.VMEM((4, 256, 512), BF16),
                pltpu.VMEM((4, 256, 128), BF16),
                pltpu.VMEM((4, 256, 512), BF16),
                pltpu.VMEM((4, 512, 128), F32),
                pltpu.VMEM((32, 128, 128), F32),
                pltpu.VMEM((32, 128, 256), F32),
                pltpu.SemaphoreType.DMA((EV_COUNT,)),
                pltpu.SemaphoreType.DMA((EV_COUNT,)),
                pltpu.SemaphoreType.DMA((10,)),
            ],
            compiler_params=pltpu.CompilerParams(
                collective_id=0, has_side_effects=True, vmem_limit_bytes=56 << 20
            ),
        )(
            clean_states[0], noise_mask, mask_embed.reshape(32, 128), queries[0],
            w_key, w_value, cosine, sine, far_cosine, far_sine,
        )
        return output[None]

    placed = (
        P("fsdp", "seq", None),
        P("fsdp", "seq"),
        P(),
        P("fsdp", "seq", None),
        P("fsdp", None),
        P("fsdp", None),
    )
    return jax.shard_map(
        shards, mesh=mesh, in_specs=placed, out_specs=P("fsdp", "seq", None), check_vma=False
    )
```

```python
import jax
import jax.numpy as jnp
import numpy as np
from jax import lax
from jax.experimental import pallas as pl
from jax.experimental.pallas import tpu as pltpu
from jax.sharding import PartitionSpec as P

MESH = pl.DeviceIdType.MESH
BF16 = jnp.bfloat16
F32 = jnp.float32
HEAD_DIM = 128
BLOCK = 256
ROPE_BASE = 500000.0
SCORE_SCALE = float(HEAD_DIM**-0.5 * np.log2(np.e))
NT = (((1,), (1,)), ((), ()))

ROUTE = {
    (0, 1, 0): "buddy", (0, 1, 1): "xl", (1, 1, 0): "buddy", (1, 1, 1): "xl",
    (0, 2, 0): "buddy", (0, 2, 1): "xl", (1, 2, 0): "xh", (1, 2, 1): "xh",
    (0, 3, 0): "buddy", (0, 3, 1): "xl", (1, 3, 0): "mate", (1, 3, 1): "xl",
    (0, 4, 0): "buddy", (0, 4, 1): "xl", (1, 4, 0): "xh", (1, 4, 1): "xh",
}
PLANE = ((0, 1), (1, 0), (3, 0), (1, 1), (3, 1), (2, 0), (2, 1))

EV_X, EV_XH, EV_Z, EV_P = 0, 1, 3, 19
EV_Q, EV_M, EV_K, EV_V, EV_O = 35, 38, 41, 49, 57
EV_COUNT = 60


def event(ring, distance, other):
    return (ring * 4 + distance - 1) * 2 + other


def kernel(
    states, marks, mask_row, queries, w_key, w_value, cosine, sine, far_cosine, far_sine, out,
    x_buf, w_buf, sums, k_own, v_own, v_relay, k_all, v_all, q_buf, m_buf, o_buf,
    tables, row_max, mix, send_sem, recv_sem, local_sem,
):
    seq = lax.axis_index("seq")
    fsdp = lax.axis_index("fsdp")
    core = seq % 2
    chip = seq // 2
    xl = chip % 2
    y = chip // 2
    z = fsdp // 2
    xh = fsdp % 2
    role = y % 2
    side = (y + xl) % 2
    mate = (3 - y) * 2 + xl

    def at(yy, xx, cc):
        return ((yy % 4 * 2 + xx) * 2 + cc, fsdp)

    near = {
        "buddy": at(y // 2 * 2 + 1 - y % 2, xl, core),
        "xl": at(y, 1 - xl, core),
        "xh": (at(y, 1 - xl, core)[0], z * 2 + 1 - xh),
        "z+": (seq, (z + 1) % 8 * 2 + xh),
        "z-": (seq, (z + 7) % 8 * 2 + xh),
        "core": at(y, xl, 1 - core),
        "mate": at(3 - y, xl, core),
        "mate2": at(3 - y, xl, 1 - core),
    }

    def remote(src, dst, number, device):
        return pltpu.make_async_remote_copy(
            src, dst, send_sem.at[number], recv_sem.at[number],
            device_id=device, device_id_type=MESH,
        )

    locals_ = []

    def local(src, dst, number):
        copy = pltpu.make_async_copy(src, dst, local_sem.at[number])
        copy.start()
        return copy

    wide = pl.ds(pl.multiple_of(core * 256, 256), 256)
    own = fsdp * 2
    load_w = []
    for half in range(2):
        rows = pl.ds(half * 128, 128)
        load_w.append(local(w_key.at[rows, wide], w_buf.at[own + half, :, pl.ds(0, 256)], half * 2))
        load_w.append(local(w_value.at[rows, wide], w_buf.at[own + half, :, pl.ds(256, 256)], half * 2 + 1))
    my_rows = pl.ds(pl.multiple_of(core * 256, 256), 256)
    load_x = local(states, x_buf.at[my_rows, :], 4)
    head = 2 * core + role
    q_cols = pl.ds(pl.multiple_of(head * 512, 512), 512)
    load_q = local(queries.at[:, q_cols], q_buf.at[core], 5)
    load_t = []
    for number, table in enumerate((cosine, sine)):
        load_t.append(local(table, tables.at[number], 6 + number))

    peers = [at(y + dy, xl if dx == 0 else 1 - xl, core) for dy, dx in PLANE]
    peers += [near["core"], near["mate2"], near["xh"], near["z+"], near["z-"]]
    barrier = pltpu.get_barrier_semaphore()
    for peer in peers:
        pl.semaphore_signal(barrier, inc=1, device_id=peer, device_id_type=MESH)
    pl.semaphore_wait(barrier, len(peers))

    sends = []

    def send(src, dst, number, device):
        copy = remote(src, dst, number, device)
        copy.start()
        sends.append(copy)

    for copy in load_w:
        copy.wait()
    other = (z * 2 + 1 - xh) * 2

    def piece(zz, flip, half):
        aa = 1 - xh if flip else xh
        return (zz % 8 * 2 + aa) * 2 + half

    def part(distance, ring):
        if distance < 4:
            return pl.ds(0, 128)
        return pl.ds(ring * 64, 64)

    def ring_send(ring, distance, flip):
        source = z - (distance - 1) if ring == 0 else z + (distance - 1)
        ref = w_buf.at[piece(source + 8, flip, side), part(distance, ring), :]
        send(ref, ref, EV_Z + event(ring, distance, flip), near["z+" if ring == 0 else "z-"])

    send(w_buf.at[own + 1 - side], w_buf.at[own + 1 - side], EV_XH, near["xh"])
    for ring in range(2):
        ring_send(ring, 1, 0)
    send(w_buf.at[own + side], w_buf.at[own + side], EV_XH + 1, near["xh"])
    send(states, x_buf.at[my_rows, :], EV_X, near["core"])

    landing = w_buf.at[other + side]
    remote(landing, landing, EV_XH, near["xh"]).wait_recv()
    for ring in range(2):
        ring_send(ring, 1, 1)

    flags = jnp.broadcast_to(marks[...].astype(F32), (128, 256))
    m_buf[core] = jnp.transpose(flags).astype(BF16)

    def q_at(kv_head):
        return queries.at[:, pl.ds(pl.multiple_of(kv_head * 512, 512), 512)]

    send(q_at(2 * (1 - core) + role), q_buf.at[core], EV_Q, near["core"])
    send(m_buf.at[core], m_buf.at[core], EV_M, near["core"])
    send(m_buf.at[core], m_buf.at[2 + core], EV_M + 1, near["mate"])
    send(m_buf.at[core], m_buf.at[2 + core], EV_M + 2, near["mate2"])

    def project(zz, first=False):
        zz = zz % 8
        weights = w_buf[pl.ds(zz * 4, 4)].reshape(512, 512)
        rows = x_buf[:, pl.ds(pl.multiple_of(zz * 512, 512), 512)]
        term = jnp.dot(rows, weights, preferred_element_type=F32)
        if first:
            sums[...] = term
        else:
            sums[...] += term

    def plane_wait(distance):
        for ring in range(2):
            source = z - distance if ring == 0 else z + distance
            for flip in range(2):
                way = ROUTE[ring, distance, flip]
                ref = w_buf.at[piece(source + 8, flip, 1 - side), part(distance, ring), :]
                remote(ref, ref, EV_P + event(ring, distance, flip), near[way]).wait_recv()

    for distance in range(1, 5):
        for flip in range(2):
            for ring in range(2):
                source = z - distance if ring == 0 else z + distance
                ref = w_buf.at[piece(source + 8, flip, side), part(distance, ring), :]
                number = event(ring, distance, flip)
                remote(ref, ref, EV_Z + number, near["z-" if ring == 0 else "z+"]).wait_recv()
                if distance < 4:
                    ring_send(ring, distance + 1, flip)
                way = ROUTE[ring, distance, flip]
                if way != "xh":
                    send(ref, ref, EV_P + number, near[way])
                elif flip == 1:
                    for mine in range(2):
                        ref = w_buf.at[piece(source + 8, 1 - mine, side), part(distance, ring), :]
                        send(ref, ref, EV_P + event(ring, distance, mine), near["xh"])
        if distance == 1:
            mask_rows = mask_row[...].astype(F32)
            for i in range(32):
                wide_row = jnp.broadcast_to(mask_rows[i : i + 1, :], (16, 128))
                x_buf[pl.ds(512, 16), pl.ds(i * 128, 128)] = wide_row.astype(BF16)

            for copy in load_t:
                copy.wait()
            near_c, near_s = tables[0], tables[1]
            for pair, where in ((1, mate), (0, chip)):
                far_c, far_s = far_cosine[pl.ds(where, 1), :], far_sine[pl.ds(where, 1), :]
                tables[pair * 2] = near_c * far_c - near_s * far_s
                tables[pair * 2 + 1] = near_s * far_c + near_c * far_s
            load_x.wait()
            theirs = x_buf.at[pl.ds(pl.multiple_of((1 - core) * 256, 256), 256), :]
            remote(theirs, theirs, EV_X, near["core"]).wait_recv()
            landing = w_buf.at[other + 1 - side]
            remote(landing, landing, EV_XH + 1, near["xh"]).wait_recv()
            project(z, True)
            send(q_at(2 * core + 1 - role), q_buf.at[2 + core], EV_Q + 1, near["mate"])
            send(q_at(2 * (1 - core) + 1 - role), q_buf.at[2 + core], EV_Q + 2, near["mate2"])
        else:
            plane_wait(distance - 1)
            project(z + 8 - distance + 1)
            project(z + distance - 1)
            if distance == 3:
                v_all[:, pl.ds(128, 128)] = jnp.ones((v_all.shape[0], 128), BF16)
                row_max[...] = jnp.full(row_max.shape, -1e30, F32)
                mix[...] = jnp.zeros(mix.shape, F32)
    plane_wait(4)
    project(z + 4)

    def rotate(rows, pair, first, count):
        turned = pltpu.roll(rows, 64, 1)
        span = pl.ds(first, count)
        return rows * tables[pair * 2, span, :] + turned * tables[pair * 2 + 1, span, :]

    for kind in range(2):
        keys = sums[pl.ds(0, 512), pl.ds(kind * 128, 128)]
        k_own[kind] = rotate(keys, 0, 0, 512).astype(BF16)
        v_own[kind] = sums[pl.ds(0, 512), pl.ds(256 + kind * 128, 128)].astype(BF16)

    def kv_rows(where):
        return pl.ds(pl.multiple_of(where * 512, 512), 512)

    def k_at(where):
        return k_all.at[kv_rows(where), :]

    def v_at(where):
        return v_all.at[kv_rows(where), pl.ds(0, 128)]

    beside = y * 2 + 1 - xl

    def seen(dy, source_y):
        return jnp.logical_not((source_y == 3) & ((dy == 2) | (dy == 3)))

    def hop(dy):
        return at(y + dy, xl, core)

    send(v_own.at[1 - role], v_relay, EV_V, near["xl"])
    send(k_own.at[role], k_at(chip), EV_K + 1, near["xl"])
    send(v_own.at[role], v_at(chip), EV_V + 1, near["xl"])

    def first_hop(dy, values):
        kind = (role + dy) % 2
        if values:
            return remote(v_own.at[kind], v_at(chip), EV_V + dy * 2, hop(dy))
        return remote(k_own.at[kind], k_at(chip), EV_K + dy * 2, hop(dy))

    def second_hop_v(dy):
        source = v_at(beside) if dy == 2 else v_relay
        return remote(source, v_at(beside), EV_V + dy * 2 + 1, hop(dy))

    def second_hop_k(dy):
        rows = k_at((y + 4 - dy) % 4 * 2 + xl)
        return remote(rows, rows, EV_K + dy * 2 + 1, near["xl"])

    for dy, values in ((1, 0), (3, 0), (1, 1), (3, 1), (2, 0), (2, 1)):
        @pl.when(seen(dy, y))
        def _():
            first_hop(dy, values).start()

    k_all[kv_rows(chip), :] = k_own[role]
    v_all[kv_rows(chip), pl.ds(0, 128)] = v_own[role]

    load_q.wait()
    for number, slot, device in (
        (EV_Q, 1 - core, near["core"]),
        (EV_Q + 1, 2 + core, near["mate"]),
        (EV_Q + 2, 3 - core, near["mate2"]),
    ):
        remote(q_buf.at[slot], q_buf.at[slot], number, device).wait_recv()
        mark = number - EV_Q + EV_M
        remote(m_buf.at[slot], m_buf.at[slot], mark, device).wait_recv()

    mask_key = sums[pl.ds(512, 16), pl.ds(pl.multiple_of(role * 128, 128), 128)]
    mask_value = sums[pl.ds(512, 16), pl.ds(pl.multiple_of(256 + role * 128, 128), 128)]
    mask_key = jnp.broadcast_to(mask_key[0:1, :], (256, 128))
    mask_value = jnp.broadcast_to(mask_value[0:1, :], (256, 128)).astype(BF16).astype(F32)

    def build(pair):
        where = mate if pair else chip
        for i in range(2):
            slot = pair * 2 + i
            base = 4096 + slot * 512
            block = pl.ds(pl.multiple_of(where * 512 + i * 256, 256), 256)
            masked = m_buf[slot].astype(F32) > 0.5
            noisy_k = jnp.where(
                masked, rotate(mask_key, pair, i * 256, 256), k_all[block, :].astype(F32)
            ).astype(BF16)
            noisy_v = jnp.where(
                masked, mask_value, v_all[block, pl.ds(0, 128)].astype(F32)
            ).astype(BF16)
            noisy = pl.ds(base + i * 256, 256)
            k_all[noisy, :] = noisy_k
            v_all[noisy, pl.ds(0, 128)] = noisy_v
            if i == 0:
                k_all[pl.ds(base + 256, 256), :] = noisy_k
                v_all[pl.ds(base + 256, 256), :] = jnp.zeros((256, 256), BF16)
            else:
                before = pl.ds(pl.multiple_of(where * 512, 512), 256)
                k_all[pl.ds(base, 256), :] = k_all[before, :]
                v_all[pl.ds(base, 256), pl.ds(0, 128)] = v_all[before, pl.ds(0, 128)]

    def absorb(slot, start):
        span = pl.ds(pl.multiple_of(start, 512), 512)
        for tile in range(8):
            query = q_buf[slot, pl.ds(tile % 2 * 128, 128), pl.ds(tile // 2 * 128, 128)]
            scores = lax.dot_general(query, k_all[span, :], NT, preferred_element_type=F32)
            before = row_max[slot * 8 + tile]
            after = jnp.maximum(before, jnp.max(scores, 1, keepdims=True))
            shrink = jnp.exp2((before - after) * SCORE_SCALE)
            probs = jnp.exp2((scores - jnp.tile(after, (1, 4))) * SCORE_SCALE).astype(BF16)
            term = jnp.dot(probs, v_all[span, :], preferred_element_type=F32)
            total = mix[slot * 8 + tile]
            mix[slot * 8 + tile] = total * jnp.tile(shrink, (1, 2)) + term
            row_max[slot * 8 + tile] = after

    def finish(slot):
        for tile in range(8):
            total = mix[slot * 8 + tile]
            o_buf[slot, pl.ds(tile % 2 * 128, 128), pl.ds(tile // 2 * 128, 128)] = (
                total[:, :128] / total[:, 128:]
            ).astype(BF16)

    out_cols = pl.ds(pl.multiple_of(head * 512, 512), 512)

    def mate_out(i):
        number = EV_O + (i - core + 2) % 2
        return remote(o_buf.at[2 + i], out.at[:, out_cols], number, at(3 - y, xl, i))

    late = (y == 0) | (y == 2)

    def source_of(turn):
        dy = jnp.where(turn >= 6, 2, jnp.where((turn == 0) | (turn == 3), 0, jnp.where((turn == 1) | (turn == 4), 1, 3)))
        dx = jnp.where((turn == 3) | (turn == 4) | (turn == 5) | (turn == 7), 1, 0)
        source_y = (y + 4 - dy) % 4
        return dy, dx, source_y, source_y * 2 + jnp.where(dx == 0, xl, 1 - xl)

    def visit(number, carry):
        turn = number % 8
        first = number < 8
        dy, dx, source_y, source = source_of(turn)
        here = first & seen(dy, source_y)
        device = near["xl"]

        def pass_on_k(hop_y):
            @pl.when(seen(hop_y, (y + 4 - hop_y) % 4))
            def _():
                rows = k_at((y + 4 - hop_y) % 4 * 2 + xl)
                remote(rows, rows, EV_K + hop_y * 2, device).wait_recv()
                second_hop_k(hop_y).start()

        def pass_on_v(hop_y):
            @pl.when(seen(hop_y, y))
            def _():
                second_hop_v(hop_y).start()

        @pl.when(number == 1)
        def _():
            remote(v_relay, v_relay, EV_V, device).wait_recv()
            pass_on_v(1)
            pass_on_v(3)
            pass_on_k(1)
            pass_on_k(3)

        @pl.when(number == 3)
        def _():
            remote(v_at(beside), v_at(beside), EV_V + 1, device).wait_recv()
            pass_on_v(2)
            pass_on_k(2)

        @pl.when(here & (dx == 1))
        def _():
            remote(k_at(source), k_at(source), EV_K + dy * 2 + 1, device).wait_recv()

        @pl.when(here & (turn != 0) & (turn != 3))
        def _():
            remote(v_at(source), v_at(source), EV_V + dy * 2 + dx, device).wait_recv()

        @pl.when(number == 0)
        def _():
            build(0)

        @pl.when(first & (source == mate))
        def _():
            build(1)

        def item(index, carry):
            both = turn == 7
            slot = (jnp.where(both, index // 2, index) + 2) % 4
            _, _, _, earlier = source_of(6)
            origin = jnp.where(both & (index % 2 == 0), earlier, source)
            other_pair = slot >= 2
            level = jnp.where(other_pair, mate, chip)
            turn_now = jnp.where(other_pair | (y >= 2), first, jnp.logical_not(first))

            @pl.when(turn_now & (origin <= level))
            def _():
                absorb(slot, jnp.where(origin == level, 4096 + slot * 512, origin * 512))

            done = number == jnp.where(late, 7, 5)

            @pl.when(other_pair & done & ((turn < 7) | (index % 2 == 1)))
            def _():
                finish(slot)
                mate_out(slot - 2).start()

            return carry

        lax.fori_loop(0, jnp.where(turn < 6, 4, jnp.where(turn == 6, 0, 8)), item, 0)
        return carry

    lax.fori_loop(0, jnp.where(y < 2, 16, 8), visit, 0)
    for i in range(2):
        finish(i)
    send(o_buf.at[1 - core], out.at[:, out_cols], EV_O + 2, near["core"])
    store = local(o_buf.at[core], out.at[:, out_cols], 5)
    store.wait()

    def o_at(kv_head):
        return out.at[:, pl.ds(pl.multiple_of(kv_head * 512, 512), 512)]

    for number, kv_head, device in (
        (EV_O, 2 * core + 1 - role, near["mate"]),
        (EV_O + 1, 2 * (1 - core) + 1 - role, near["mate2"]),
        (EV_O + 2, 2 * (1 - core) + role, near["core"]),
    ):
        remote(o_at(kv_head), o_at(kv_head), number, device).wait_recv()
    for i in range(2):
        mate_out(i).wait_send()
    for dy in (1, 2, 3):
        @pl.when(seen(dy, y))
        def _():
            for values in range(2):
                first_hop(dy, values).wait_send()
            second_hop_v(dy).wait_send()

        @pl.when(seen(dy, (y + 4 - dy) % 4))
        def _():
            second_hop_k(dy).wait_send()
    for copy in sends:
        copy.wait_send()


def tables_of(positions):
    half = HEAD_DIM // 2
    steps = np.arange(half, dtype=np.float32) * np.float32(2.0) / np.float32(HEAD_DIM)
    frequency = (np.float32(ROPE_BASE) ** (-steps)).astype(np.float64)
    angles = positions.astype(np.float64)[:, None] * frequency[None, :]
    cosine = np.cos(angles).astype(np.float32)
    sine = np.sin(angles).astype(np.float32)
    return jnp.asarray(np.concatenate([cosine, cosine], 1)), jnp.asarray(np.concatenate([-sine, sine], 1))


def solution(mesh):
    def shards(clean_states, noise_mask, mask_embed, queries, w_key, w_value):
        _, rows, width = clean_states.shape
        cosine, sine = tables_of(np.arange(2 * rows))
        far_cosine, far_sine = tables_of(np.arange(8) * 2 * rows)
        any_ = pl.BlockSpec(memory_space=pl.ANY)
        vmem = pl.BlockSpec(memory_space=pltpu.VMEM)
        output = pl.pallas_call(
            kernel,
            out_shape=pltpu.VMEM((256, 2048), BF16),
            in_specs=[any_, vmem, vmem, any_, any_, any_, any_, any_, vmem, vmem],
            out_specs=vmem,
            scratch_shapes=[
                pltpu.VMEM((528, 4096), BF16),
                pltpu.VMEM((32, 128, 512), BF16),
                pltpu.VMEM((528, 512), F32),
                pltpu.VMEM((2, 512, 128), BF16),
                pltpu.VMEM((2, 512, 128), BF16),
                pltpu.VMEM((512, 128), BF16),
                pltpu.VMEM((6144, 128), BF16),
                pltpu.VMEM((6144, 256), BF16),
                pltpu.VMEM((4, 256, 512), BF16),
                pltpu.VMEM((4, 256, 128), BF16),
                pltpu.VMEM((4, 256, 512), BF16),
                pltpu.VMEM((4, 512, 128), F32),
                pltpu.VMEM((32, 128, 128), F32),
                pltpu.VMEM((32, 128, 256), F32),
                pltpu.SemaphoreType.DMA((EV_COUNT,)),
                pltpu.SemaphoreType.DMA((EV_COUNT,)),
                pltpu.SemaphoreType.DMA((10,)),
            ],
            compiler_params=pltpu.CompilerParams(
                collective_id=0, has_side_effects=True, vmem_limit_bytes=56 << 20
            ),
        )(
            clean_states[0], noise_mask, mask_embed.reshape(32, 128), queries[0],
            w_key, w_value, cosine, sine, far_cosine, far_sine,
        )
        return output[None]

    placed = (
        P("fsdp", "seq", None),
        P("fsdp", "seq"),
        P(),
        P("fsdp", "seq", None),
        P("fsdp", None),
        P("fsdp", None),
    )
    return jax.shard_map(
        shards, mesh=mesh, in_specs=placed, out_specs=P("fsdp", "seq", None), check_vma=False
    )
```
